32 devices in a mesh: groups: 2 (over y), feat: 4 (over z), layer: 2 (over x), tok: 2 (over core).
Axes of the slice: x: 2, y: 2, z: 4, core: 2. Of those that a mesh axis runs over, the one named last changes fastest.
Arguments:
- residual_in: float32 [256, 2, 1792], P('groups', 'tok', 'feat'), parts along dimension 0, may hold values from -6 to 6
- attn_scale: float32 [2, 256], P('layer', 'groups'), parts along dimension 1, may hold values from 0.4 to 2.5
- mlp_scale: float32 [2, 256], P('layer', 'groups'), parts along dimension 1, may hold values from 0.4 to 2.5
- patterns: bfloat16 [2, 8, 4, 64, 64], P('layer', None, 'groups'), parts along dimension 2, may hold values from 0.0029907227 to 0.059814453
- lengths: int32 [4], P('groups'), parts along dimension 0, may hold values from 16 to 64
- value_proj: bfloat16 [2, 2, 1792, 1024], P('layer', 'tok', None, 'feat'), may hold values from -0.09375 to 0.09375
- out_proj: bfloat16 [2, 4, 256, 2, 2, 1792], P('layer', None, None, None, 'tok', 'feat'), may hold values from -0.125 to 0.125
- enc_weight: bfloat16 [2, 2, 1792, 512], P('layer', 'tok', None, 'feat'), may hold values from -0.09375 to 0.09375
- enc_bias: float32 [2, 512], P('layer', 'feat'), may hold values from -3 to 3
- dec_weight: bfloat16 [2, 2, 512, 2, 1792], P('layer', None, None, 'tok', 'feat'), may hold values from -0.25 to 0.25
- errors: float32 [2, 256, 2, 1792], P('layer', 'groups', 'tok', 'feat'), parts along dimension 1, may hold values from -4 to 4
- clamp_mode: int32 [2, 16384], P('layer', 'feat'), may hold values from 0 to 2
- clamp_index: int32 [2, 16384], P('layer', 'feat'), may hold values from 0 to 63
- clamp_values: float32 [64], replicated, may hold values from 0.25 to 3
- active_blocks: int32 [2, 4], P('layer', 'feat'), may hold values from 0 to 31
Outputs:
- residual_out: float32 [2, 256, 2, 1792], P('layer', 'groups', 'tok', 'feat'), parts along dimension 1
- features: bfloat16 [2, 256, 512], P('layer', 'groups', 'feat'), parts along dimension 1
The draws below stay inside these ranges and needn't reach their ends.
There are 2 independent parts, one for each index of `groups`. The reference program is written for one: setup_inputs(seed, part) draws one part's arguments, and reference() takes and returns one part's arrays. A program takes and returns all parts, laid end to end along the dimension named above; an argument that names none is the same for every part. Nothing has to cross between parts.
Inputs may be any that keep to these rules, and one draw needn't show every extreme that they name: `clamp_mode`: 0 leaves a feature free, 1 sets it to its table value, 2 multiplies it by its table value. `lengths`: positions at or past a prompt's length are padding.
All inputs are finite; a program needn't handle non-finite values.
Results may differ from the reference program's by a relative error of at most 0.018.
Values may be sent and summed in bfloat16 or wider, within the bound.
A program may use at most 64 MiB of HBM per device.

```python
import math
import jax
import jax.numpy as jnp

D = 3584
HD = 256
HEADS = 8
KVH = 4
FEATURES = 16384
BLOCK = 128
VALUES = 64
SEQ = 64
PROMPTS = 2
QPK = 2
LAYERS = 2
RANGES = 4
ACT = 512
SHARD_BLOCKS = 32
SLABS = 2
SLAB = 1792
ROWS = 128


def place_ends(values, stream_key, low, high):
    spot = [jax.random.randint(jax.random.fold_in(stream_key, axis), (), 0, length) for axis, length in enumerate(values.shape)]
    widest = values.shape.index(max(values.shape))
    neighbour = spot[:widest] + [(spot[widest] + 1) % values.shape[widest]] + spot[widest + 1:]
    return values.at[tuple(spot)].set(low).at[tuple(neighbour)].set(high)


def level_of(key, shape, pieces, smallest, top_value):
    def one(axis_at, shards_of):
        draws = jax.random.uniform(jax.random.fold_in(jax.random.fold_in(key, 6), axis_at), (shards_of,), jnp.float32, smallest / len(pieces), top_value / len(pieces))
        return jnp.repeat(jnp.exp(draws), shape[axis_at] // shards_of).reshape((-1,) + (1,) * (len(shape) - axis_at - 1))

    factor_of = one(*pieces[0])
    for cut in pieces[1:]:
        factor_of = factor_of * one(*cut)
    return factor_of


def normal_values(own_key, shape, scale, limit, cuts=(), kind=jnp.bfloat16):
    values = jax.random.normal(own_key, shape, jnp.float32) * scale
    if len(cuts) > 0:
        values = level_of(own_key, shape, cuts, -0.22, 0.18) * values
    return jnp.clip(values, min=-limit, max=limit).astype(kind)


def setup_inputs(seed: int = 0, part: int = 0) -> dict:
    keys = jax.random.split(jax.random.key(seed), 16)
    own_keys = jax.random.split(jax.random.fold_in(keys[15], part), 16)
    return {
        "residual_in": normal_values(own_keys[0], (ROWS, SLABS, SLAB), 1.0, 6.0, ((1, 2), (2, 4)), jnp.float32),
        "attn_scale": jnp.clip(jnp.exp(math.log(2.5) - 1.8325814 * jax.random.uniform(own_keys[1], (LAYERS, ROWS), jnp.float32) ** level_of(own_keys[1], (LAYERS, ROWS), ((0, 2),), -0.2, 0.2)), 0.4, 2.5),
        "mlp_scale": jnp.clip(jnp.exp(math.log(2.5) - 1.8325814 * jax.random.uniform(own_keys[2], (LAYERS, ROWS), jnp.float32) ** level_of(own_keys[2], (LAYERS, ROWS), ((0, 2),), -0.2, 0.2)), 0.4, 2.5),
        "patterns": jnp.clip(jnp.exp(math.log(0.059814453) - 2.9957323 * jax.random.uniform(own_keys[3], (LAYERS, HEADS, PROMPTS, SEQ, SEQ), jnp.float32) ** level_of(own_keys[3], (LAYERS, HEADS, PROMPTS, SEQ, SEQ), ((0, 2),), -0.2, 0.2)), 0.0029907227, 0.059814453).astype(jnp.bfloat16),
        "lengths": jax.random.randint(own_keys[4], (PROMPTS,), SEQ // 4, SEQ + 1).astype(jnp.int32),
        "value_proj": normal_values(keys[5], (LAYERS, SLABS, SLAB, KVH * HD), D ** -0.5, 0.09375, ((0, 2), (1, 2), (3, 4))),
        "out_proj": normal_values(keys[6], (LAYERS, KVH, HD, QPK, SLABS, SLAB), (HEADS * HD) ** -0.5, 0.125, ((0, 2), (4, 2), (5, 4))),
        "enc_weight": normal_values(keys[7], (LAYERS, SLABS, SLAB, ACT), D ** -0.5, 0.09375, ((0, 2), (1, 2), (3, 4))),
        "enc_bias": normal_values(keys[8], (LAYERS, ACT), 0.5, 3.0, ((0, 2), (1, 4)), jnp.float32),
        "dec_weight": normal_values(keys[9], (LAYERS, LAYERS, ACT, SLABS, SLAB), ACT ** -0.5, 0.25, ((0, 2), (3, 2), (4, 4))),
        "errors": normal_values(own_keys[10], (LAYERS, ROWS, SLABS, SLAB), 0.5, 4.0, ((0, 2), (2, 2), (3, 4)), jnp.float32),
        "clamp_mode": place_ends(jax.random.randint(keys[11], (LAYERS, FEATURES), 0, 3), jax.random.fold_in(keys[11], 1), 0, 2).astype(jnp.int32),
        "clamp_index": place_ends(jax.random.randint(keys[12], (LAYERS, FEATURES), 0, VALUES), jax.random.fold_in(keys[12], 1), 0, VALUES - 1).astype(jnp.int32),
        "clamp_values": jnp.clip(jax.random.uniform(keys[13], (VALUES,), jnp.float32, 0.25, 3.0), 0.25, 3.0),
        "active_blocks": place_ends(jax.random.randint(keys[14], (LAYERS, RANGES), 0, SHARD_BLOCKS), jax.random.fold_in(keys[14], 1), 0, SHARD_BLOCKS - 1).astype(jnp.int32),
    }


def pick_block(lookup_table, chosen):
    shaped = lookup_table.reshape(RANGES, SHARD_BLOCKS, BLOCK)
    taken = jnp.take_along_axis(shaped, chosen.astype(jnp.int32)[:, None, None], axis=1)
    return taken[:, 0, :].reshape(ACT)


def reference(residual_in, attn_scale, mlp_scale, patterns, lengths, value_proj, out_proj, enc_weight, enc_bias, dec_weight, errors, clamp_mode, clamp_index, clamp_values, active_blocks):
    positions = jnp.arange(SEQ, dtype=jnp.int32)
    live_rows = (positions[None, :] < lengths[:, None]).reshape(ROWS)
    keep_keys = (positions[None, None, :] <= positions[None, :, None]) & (positions[None, None, :] < lengths[:, None, None])
    state = residual_in.reshape(ROWS, D)
    feature_list = []
    state_list = []
    for layer_num in range(LAYERS):
        normed = (state * attn_scale[layer_num][:, None]).astype(jnp.bfloat16)
        values = jnp.dot(normed, value_proj[layer_num].reshape(D, KVH * HD), preferred_element_type=jnp.float32).astype(jnp.bfloat16)
        value_grid = values.reshape(PROMPTS, SEQ, KVH, HD).astype(jnp.float32)
        pattern_grid = jnp.where(keep_keys[None], patterns[layer_num].astype(jnp.float32), 0.0).reshape(KVH, QPK, PROMPTS, SEQ, SEQ)
        head_out = jnp.einsum("gupqk,pkgd->pqgdu", pattern_grid, value_grid).astype(jnp.bfloat16).reshape(ROWS, KVH * HD * QPK)
        attention = jnp.dot(head_out, out_proj[layer_num].reshape(KVH * HD * QPK, D), preferred_element_type=jnp.float32)
        middle = state + attention
        normed_mlp = (middle * mlp_scale[layer_num][:, None]).astype(jnp.bfloat16)
        preact = jnp.dot(normed_mlp, enc_weight[layer_num].reshape(D, ACT), preferred_element_type=jnp.float32) + enc_bias[layer_num]
        active = jnp.maximum(preact, 0.0)
        modes = pick_block(clamp_mode[layer_num], active_blocks[layer_num])
        levels = clamp_values[pick_block(clamp_index[layer_num], active_blocks[layer_num])]
        clamped = jnp.where(modes == 1, levels, jnp.where(modes == 2, active * levels, active))
        features = jnp.where(live_rows[:, None], clamped, 0.0).astype(jnp.bfloat16)
        feature_list.append(features)
        recon = jnp.zeros((ROWS, D), jnp.float32)
        for source_num in range(layer_num + 1):
            recon = recon + jnp.dot(feature_list[source_num], dec_weight[source_num, layer_num].reshape(ACT, D), preferred_element_type=jnp.float32)
        state = middle + recon + errors[layer_num].reshape(ROWS, D)
        state_list.append(state)
    return jnp.stack(state_list).reshape(LAYERS, ROWS, SLABS, SLAB), jnp.stack(feature_list)
```

```python
import functools

import jax
import jax.numpy as jnp
from jax import lax
from jax.experimental import pallas as pl
from jax.experimental.pallas import tpu as pltpu
from jax.sharding import PartitionSpec as P

F32 = jnp.float32
BF16 = jnp.bfloat16
NT = (((1,), (1,)), ((), ()))


def column(row):
    rows = row.shape[1]
    return jnp.transpose(jnp.broadcast_to(row, (128, rows)))[:, 0:1]


def kernel(
    sizes,
    lengths_in, table_in, chosen_in, attn_in, mlp_in, bias_in, mode_in, index_in,
    x_in, err_in, pat_in, wv_in, wo_in, we_in, wd_in,
    out_ref, feat_ref,
    lengths, table, chosen, scale_attn, scale_mlp, bias, mode_row, index_row,
    x_t, err_t, pat, wv, wo, we, wd,
    xbuf, slots, relay_x, nbuf, masked, part_v, part_v2, vals, part_e, e_out, e_in, feats,
    acc_in, acc_out, att, err, wek, relay_in, relay_mid,
    local_sem, xs_send, xs_recv, rx_send, ns_send, zx_send, zx_recv, zf_send, t_send, t_recv,
    v_send, v_recv, vf_send, m_send, m_recv, f_send, f_recv, a_send, a_recv,
    w_send, w_recv, b_send, b_recv,
):
    layers, feat_n, seq, prompts, head_dim, per_group, kv, width, block, rows, entries, shares = sizes
    half = seq // 2
    me_g = lax.axis_index("groups")
    me_l = lax.axis_index("layer")
    me_f = lax.axis_index("feat")
    me_t = lax.axis_index("tok")
    has_next = me_l < layers - 1
    has_prev = me_l > 0
    is_first = jnp.logical_not(has_prev)
    other = 1 - me_t
    nxt = jnp.minimum(me_l + 1, layers - 1)
    prv = jnp.maximum(me_l - 1, 0)
    streams = range(prompts)
    ends = (0, feat_n - 1)
    at_end = jnp.logical_or(me_f == 0, me_f == feat_n - 1)
    order = sorted(range(feat_n), key=lambda s: abs(2 * s - feat_n + 1))
    low_side = 2 * me_f < feat_n
    both = jnp.logical_and

    loads = [
        pltpu.make_async_copy(src, dst, local_sem.at[i])
        for i, (src, dst) in enumerate(
            (
                (x_in, x_t), (we_in, we), (attn_in, scale_attn), (lengths_in, lengths), (table_in, table),
                (chosen_in, chosen), (mlp_in, scale_mlp), (bias_in, bias), (mode_in, mode_row),
                (index_in, index_row), (wv_in, wv), (pat_in, pat), (wo_in, wo), (wd_in, wd), (err_in, err_t),
            )
        )
    ]
    for load in loads:
        load.start()
    l_x, l_we = loads[:2]

    barrier = pltpu.get_barrier_semaphore()
    mesh_id = pl.DeviceIdType.MESH

    def greet(where):
        pl.semaphore_signal(barrier, inc=1, device_id=where, device_id_type=mesh_id)

    for j in range(1, feat_n):
        for t in range(2):
            greet({"feat": (me_f + j) % feat_n, "tok": t})
    pl.when(has_next)(lambda: greet({"layer": nxt}))
    pl.when(has_prev)(lambda: greet({"layer": prv}))
    for g in range(1, shares):
        pl.when(is_first)(lambda: greet({"groups": (me_g + g) % shares, "layer": nxt}))
        pl.when(me_l == 1)(lambda: greet({"groups": (me_g + g) % shares, "layer": prv}))
    greet({"tok": other})

    def send(src, dst, ss, rs, where):
        return pltpu.make_async_remote_copy(
            src_ref=src, dst_ref=dst, send_sem=ss, recv_sem=rs, device_id=where, device_id_type=mesh_id
        )

    def peer(j):
        return (me_f + j) % feat_n

    def far(k):
        down = feat_n - 1 - k
        return jnp.where(low_side, down - jnp.where(down <= me_f, 1, 0), k + jnp.where(k >= me_f, 1, 0))

    def part(p):
        return pl.ds(p * seq, seq)

    pending = []

    def launch(copy, cond=None):
        pending.append((copy, cond))
        if cond is None:
            copy.start()
        else:
            pl.when(cond)(copy.start)

    def landed(ref, ss, rs):
        send(ref, ref, ss, rs, {"tok": other}).wait_recv()

    l_x.wait()
    x_rows = jnp.transpose(x_t[...])

    @pl.when(is_first)
    def _():
        x_half = x_rows.astype(BF16)
        for p in streams:
            slots[p, me_f] = x_half[p * seq : (p + 1) * seq]
            xbuf[p] = x_rows[p * seq : (p + 1) * seq]

    extra = (shares - 1) * (1 - jnp.minimum(me_l // 2, 1))
    pl.semaphore_wait(
        barrier, 2 * feat_n - 1 + jnp.minimum(me_l, 1) + jnp.minimum(layers - 1 - me_l, 1) + extra
    )

    def share_x(p, step, cond):
        to = me_f + step
        cond = both(both(to >= 0, to < feat_n), cond)
        to = jnp.clip(to, 0, feat_n - 1)
        slot = slots.at[p, me_f]
        launch(send(slot, slot, xs_send.at[p, to], xs_recv.at[p, me_f], {"feat": to}), cond)

    def x_landed(p, s):
        landed(slots.at[p, s], xs_send.at[p, 0], xs_recv.at[p, s])

    for p in streams:
        for step in (2, -2, 1, -1):
            share_x(p, step, is_first)

    def we_rows(s):
        return we.at[pl.ds(pl.multiple_of(s * width, 16), width)]

    l_we.wait()
    own_rows = pltpu.make_async_copy(we_rows(me_f), wek.at[me_f], local_sem.at[len(loads)])
    own_rows.start()
    share = width // shares
    my_share = me_g if shares > 1 else 0
    front = pl.ds(0, share)
    first_up = [
        send(
            we.at[pl.ds(pl.multiple_of(peer(j) * width + my_share * share, 16), share)],
            relay_in.at[peer(j), front], w_send.at[0, j], w_recv.at[0, peer(j)], {"layer": nxt},
        )
        for j in range(1, feat_n)
    ]
    across = [
        send(
            relay_in.at[peer(j), front], relay_mid.at[me_f, front],
            w_send.at[1, j], w_recv.at[1, me_f], {"feat": peer(j)},
        )
        for j in range(1, feat_n)
    ]
    back = [
        [
            send(
                relay_mid.at[peer(j), front],
                wek.at[peer(j), pl.ds(pl.multiple_of(my_share * share, 16), share)],
                b_send.at[g, j], b_recv.at[my_share, peer(j)],
                {"layer": prv, "groups": (me_g + g) % shares} if g else {"layer": prv},
            )
            for g in range(shares)
        ]
        for j in range(1, feat_n)
    ]
    direct = [
        send(we_rows(peer(j)), wek.at[me_f], w_send.at[3, j], w_recv.at[2, me_f], {"feat": peer(j)})
        for j in range(1, feat_n)
    ]

    def w_arrived(ref, stage, s):
        part_ref = ref.at[s, front] if stage < 2 else ref.at[s]
        send(part_ref, part_ref, w_send.at[stage, 0], w_recv.at[stage, s], {"tok": other}).wait_recv()

    @pl.when(is_first)
    def _():
        for copy in first_up:
            copy.start()

    @pl.when(me_l == 1)
    def _():
        for j in range(1, feat_n):
            w_arrived(relay_in, 0, peer(j))
            across[j - 1].start()
        for j in range(1, feat_n):
            w_arrived(relay_mid, 1, peer(j))
            for copy in back[j - 1]:
                copy.start()

    @pl.when(has_prev)
    def _():
        for copy in direct:
            copy.start()

    for load in loads[2:]:
        load.wait()
    ids = lax.broadcasted_iota(jnp.int32, (half, 1), 0) + me_t * half
    lives = [ids < lengths[p] for p in streams]
    which = jnp.zeros((1, block), jnp.int32) + chosen[0, 0]
    modes = picks = jnp.zeros((1, block), jnp.int32)
    for b in range(mode_row.shape[1] // block):
        here = which == b
        modes = jnp.where(here, mode_row[:, b * block : (b + 1) * block], modes)
        picks = jnp.where(here, index_row[:, b * block : (b + 1) * block], picks)
    levels = jnp.zeros((1, block), F32)
    for v in range(entries):
        levels = jnp.where(picks == v, table[v], levels)
    attn_col = column(scale_attn[...])
    mlp_col = column(scale_mlp[...])
    shift = bias[...]
    err[...] = jnp.transpose(err_t[...])
    q_ids = lax.broadcasted_iota(jnp.int32, (seq, seq), 0)
    k_ids = lax.broadcasted_iota(jnp.int32, (seq, seq), 1)
    for p in streams:
        keep = both(k_ids <= q_ids, k_ids < lengths[p])
        for h in range(pat.shape[0]):
            masked[h // per_group, p, pl.ds(h % per_group * seq, seq), :] = jnp.where(
                keep, pat[h, p].astype(F32), 0.0
            ).astype(BF16)
        e_in[p, me_f, me_t] = jnp.zeros((half, block), BF16)
    own_rows.wait()

    for p in streams:
        @pl.when(has_prev)
        def _():
            x_landed(p, me_f)
            xbuf[p] = slots[p, me_f].astype(F32)

        for k in range(1, feat_n):
            for step in (feat_n - k, k - feat_n):
                share_x(p, step, has_prev if abs(step) == 1 else both(has_prev, jnp.logical_not(at_end)))

    for p in streams:
        total = jnp.zeros((seq, kv), F32)
        for s in order:
            pl.when(me_f != s)(lambda: x_landed(p, s))
            for side, step in enumerate((1, -1)):
                to = me_f + step
                inside = both(to >= 0, to < feat_n)
                if_far = (to - s) * step > 2
                launch(
                    send(
                        slots.at[p, s], slots.at[p, s], rx_send.at[p, s, side], xs_recv.at[p, s],
                        {"feat": jnp.clip(to, 0, feat_n - 1)},
                    ),
                    both(is_first, both(inside, if_far)),
                )
            total += jnp.dot(slots[p, s], wv[pl.ds(s * width, width), :], preferred_element_type=F32)
        total *= attn_col[p * seq : (p + 1) * seq]
        part_v[p] = total.reshape(2, half, kv)
        launch(send(part_v.at[p, other], part_v2.at[p], t_send.at[p], t_recv.at[p], {"tok": other}))
        landed(part_v2.at[p], t_send.at[p], t_recv.at[p])
        vals[p, me_f, me_t] = (part_v[p, me_t] + part_v2[p]).astype(BF16)
        mine = vals.at[p, me_f, me_t]
        for k in range(feat_n - 1):
            launch(send(mine, mine, v_send.at[p, k], v_recv.at[p, me_f, me_t], {"feat": far(k)}))
        launch(send(mine, mine, vf_send.at[p, me_f], v_recv.at[p, me_f, me_t], {"tok": other}))

    def take(p, s):
        got = vals.at[p, s, me_t]

        @pl.when(me_f != s)
        def _():
            landed(got, vf_send.at[p, s], v_recv.at[p, s, me_t])
            send(got, got, vf_send.at[p, s], v_recv.at[p, s, me_t], {"tok": other}).start()

        pending.append((send(got, got, vf_send.at[p, s], v_recv.at[p, s, me_t], {"tok": other}), me_f != s))

    for p in streams:
        total = jnp.zeros((seq, width), F32)
        for n in range(feat_n + 1):
            if n < feat_n:
                take(p, order[n])
            if n == 0:
                continue
            s = order[n - 1]
            landed(vals.at[p, s, other], vf_send.at[p, s], v_recv.at[p, s, other])
            group = s * kv // head_dim
            d0 = s * kv % head_dim
            heads = jnp.dot(masked[group, p], vals[p, s].reshape(seq, kv), preferred_element_type=F32).astype(BF16)
            for u in range(per_group):
                total += lax.dot_general(
                    heads[u * seq : (u + 1) * seq], wo[group, u, :, pl.ds(d0, kv)], NT, preferred_element_type=F32
                )

        if p == 0:
            for s in range(feat_n):
                @pl.when(both(has_prev, me_f != s))
                def _():
                    w_arrived(wek, 2, s)

                @pl.when(both(is_first, me_f != s))
                def _():
                    for g in range(shares):
                        here = wek.at[s, pl.ds(g * share, share)]
                        send(here, here, b_send.at[0, 0], b_recv.at[g, s], {"tok": other}).wait_recv()

        middle = xbuf[p] + total
        normed_mlp = (middle * mlp_col[p * seq : (p + 1) * seq]).astype(BF16)
        for k in range(feat_n):
            to = far(k) if k < feat_n - 1 else me_f
            result = jnp.dot(normed_mlp, wek[to], preferred_element_type=F32).reshape(2, half, block)
            e_out[p, k] = result.astype(BF16)
            if k < feat_n - 1:
                for t in range(2):
                    launch(
                        send(
                            e_out.at[p, k, t], e_in.at[p, me_f, me_t], m_send.at[p, k, t],
                            m_recv.at[p, me_f, me_t], {"feat": to, "tok": t},
                        )
                    )
            else:
                part_e[p] = result
                launch(
                    send(
                        e_out.at[p, k, other], e_in.at[p, me_f, me_t], m_send.at[p, k, 0],
                        m_recv.at[p, me_f, me_t], {"tok": other},
                    )
                )
        att[part(p), :] = middle + err[part(p), :]

    def await_others(ref, ss, rs, p, s):
        for t in range(2):
            pl.when(jnp.logical_or(me_f != s, me_t != t))(
                lambda: landed(ref.at[p, s, t], ss.at[p, 0, 0], rs.at[p, s, t])
            )

    for p in streams:
        for s in order:
            await_others(e_in, m_send, m_recv, p, s)
        preact = part_e[p, me_t] + shift
        for s in range(feat_n):
            for t in range(2):
                preact += e_in[p, s, t].astype(F32)
        active = jnp.maximum(preact, 0.0)
        clamped = jnp.where(modes == 1, levels, jnp.where(modes == 2, active * levels, active))
        feats[p, me_f, me_t] = jnp.where(lives[p], clamped, 0.0).astype(BF16)
        mine = feats.at[p, me_f, me_t]
        for k in range(feat_n - 1):
            for t in range(2):
                launch(
                    send(mine, mine, f_send.at[p, k, t], f_recv.at[p, me_f, me_t], {"feat": far(k), "tok": t})
                )
        launch(send(mine, mine, f_send.at[p, feat_n - 1, 0], f_recv.at[p, me_f, me_t], {"tok": other}))

    def acc_copy(p, t):
        return send(acc_out.at[p, t], acc_in.at[p, t], a_send.at[p, t], a_recv.at[p, t], {"layer": nxt})

    for p in streams:
        @pl.when(has_prev)
        def _():
            for t in range(1, layers):
                @pl.when(t >= me_l)
                def _():
                    acc_copy(p, t).wait_recv()
            att[part(p), :] += acc_in[p, me_l]

        total = att[part(p), :]
        for s in order:
            await_others(feats, f_send, f_recv, p, s)
            total += lax.dot_general(
                feats[p, s].reshape(seq, block), wd[me_l, :, pl.ds(s * block, block)], NT,
                preferred_element_type=F32,
            )
        att[part(p), :] = total
        feat_ref[part(p), :] = feats[p, me_f].reshape(seq, block)

        @pl.when(has_next)
        def _():
            nbuf[p] = att[part(p), :].astype(BF16)

        for k in range(feat_n - 2):
            to = jnp.where(me_f == 0, feat_n - 1 - k, k)
            launch(
                send(
                    nbuf.at[p], relay_x.at[p, jnp.minimum(me_f, 1)], zx_send.at[p, k],
                    zx_recv.at[p, jnp.minimum(me_f, 1)], {"feat": to},
                ),
                both(has_next, at_end),
            )
        launch(send(nbuf.at[p], slots.at[p, me_f], ns_send.at[p], xs_recv.at[p, me_f], {"layer": nxt}), has_next)

    for p in streams:
        for e, src in enumerate(ends):
            relays = both(has_next, jnp.abs(me_f - src) > 1)
            pl.when(relays)(lambda: landed(relay_x.at[p, e], zx_send.at[p, 0], zx_recv.at[p, e]))
            launch(
                send(relay_x.at[p, e], slots.at[p, src], zf_send.at[p, e], xs_recv.at[p, src], {"layer": nxt}),
                relays,
            )

    @pl.when(has_next)
    def _():
        for p in streams:
            for t in range(1, layers):
                @pl.when(t > me_l)
                def _():
                    rest = att[part(p), :] - nbuf[p].astype(F32)
                    total = jnp.where(me_l + 1 == t, rest, 0.0)
                    for s in range(feat_n):
                        total += lax.dot_general(
                            feats[p, s].reshape(seq, block), wd[t, :, pl.ds(s * block, block)], NT,
                            preferred_element_type=F32,
                        )
                    acc_out[p, t] = total

                    @pl.when(has_prev)
                    def _():
                        acc_out[p, t] += acc_in[p, t]

                    acc_copy(p, t).start()

    out_ref[...] = jnp.transpose(att[...])

    @pl.when(is_first)
    def _():
        for copy in first_up:
            copy.wait_send()

    @pl.when(me_l == 1)
    def _():
        for copy in sum(back, across):
            copy.wait_send()

    @pl.when(has_prev)
    def _():
        for copy in direct:
            copy.wait_send()

    for copy, cond in pending:
        if cond is None:
            copy.wait_send()
        else:
            pl.when(cond)(copy.wait_send)

    @pl.when(has_next)
    def _():
        for p in streams:
            for t in range(1, layers):
                @pl.when(t > me_l)
                def _():
                    acc_copy(p, t).wait_send()


def store(x_ref, f_ref, out_ref, feat_ref, sems):
    copies = [
        pltpu.make_async_copy(x_ref, out_ref, sems.at[0]),
        pltpu.make_async_copy(f_ref, feat_ref, sems.at[1]),
    ]
    for copy in copies:
        copy.start()
    for copy in copies:
        copy.wait()


def local(
    residual_in, attn_scale, mlp_scale, patterns, lengths, value_proj, out_proj, enc_weight, enc_bias,
    dec_weight, errors, clamp_mode, clamp_index, clamp_values, active_blocks,
):
    layers = lax.axis_size("layer")
    feat_n = lax.axis_size("feat")
    prompts, seq = patterns.shape[2], patterns.shape[3]
    head_dim, per_group = out_proj.shape[2], out_proj.shape[3]
    kv = value_proj.shape[3]
    rows, _, width = residual_in.shape
    block = enc_bias.shape[1]
    entries = clamp_values.shape[0]
    groups = lax.axis_size("groups")
    shares = groups if width % (16 * groups) == 0 else 1
    sizes = (layers, feat_n, seq, prompts, head_dim, per_group, kv, width, block, rows, entries, shares)
    x_in = residual_in[:, 0, :].T
    err_in = errors[0, :, 0, :].T
    pat_in = patterns[0]
    wv_in = value_proj[0, 0]
    wo_in = jnp.transpose(out_proj[0, :, :, :, 0, :], (0, 2, 3, 1))
    we_in = enc_weight[0, 0]
    wd_in = jnp.transpose(dec_weight[0, :, :, 0, :], (0, 2, 1))
    smem = pltpu.SMEM
    vmem = pl.BlockSpec(memory_space=pltpu.VMEM)
    hbm = pl.BlockSpec(memory_space=pl.ANY)
    small = (lengths, clamp_values, active_blocks, attn_scale, mlp_scale, enc_bias, clamp_mode, clamp_index)
    big = (x_in, err_in, pat_in, wv_in, wo_in, we_in, wd_in)
    half = seq // 2
    kv_heads = out_proj.shape[1]
    dma = pltpu.SemaphoreType.DMA
    out_t, out_f = pl.pallas_call(
        functools.partial(kernel, sizes),
        out_shape=(pltpu.VMEM((width, rows), F32), pltpu.VMEM((rows, block), BF16)),
        in_specs=[hbm] * 15,
        out_specs=(vmem, vmem),
        scratch_shapes=[(smem if i < 3 else pltpu.VMEM)(a.shape, a.dtype) for i, a in enumerate(small)]
        + [pltpu.VMEM(a.shape, a.dtype) for a in big]
        + [
            pltpu.VMEM((prompts, seq, width), F32),
            pltpu.VMEM((prompts, feat_n, seq, width), BF16),
            pltpu.VMEM((prompts, 2, seq, width), BF16),
            pltpu.VMEM((prompts, seq, width), BF16),
            pltpu.VMEM((kv_heads, prompts, per_group * seq, seq), BF16),
            pltpu.VMEM((prompts, 2, half, kv), F32),
            pltpu.VMEM((prompts, half, kv), F32),
            pltpu.VMEM((prompts, feat_n, 2, half, kv), BF16),
            pltpu.VMEM((prompts, 2, half, block), F32),
            pltpu.VMEM((prompts, feat_n, 2, half, block), BF16),
            pltpu.VMEM((prompts, feat_n, 2, half, block), BF16),
            pltpu.VMEM((prompts, feat_n, 2, half, block), BF16),
            pltpu.VMEM((prompts, layers, seq, width), F32),
            pltpu.VMEM((prompts, layers, seq, width), F32),
            pltpu.VMEM((rows, width), F32),
            pltpu.VMEM((rows, width), F32),
        ]
        + [pltpu.VMEM((feat_n, width, block), BF16)] * 3
        + [dma((16,))]
        + [dma((prompts, feat_n))] * 2
        + [dma((prompts, feat_n, 2)), dma((prompts,)), dma((prompts, feat_n)), dma((prompts, 2)), dma((prompts, 2))]
        + [dma((prompts,))] * 2
        + [dma((prompts, feat_n)), dma((prompts, feat_n, 2)), dma((prompts, feat_n))]
        + [dma((prompts, feat_n, 2))] * 4
        + [dma((prompts, layers))] * 2
        + [dma((4, feat_n)), dma((3, feat_n))]
        + [dma((shares, feat_n))] * 2,
        compiler_params=pltpu.CompilerParams(collective_id=0, has_side_effects=True),
    )(*small, *big)
    out_t, out_f = pl.pallas_call(
        store,
        out_shape=(
            jax.ShapeDtypeStruct((width, rows), F32),
            jax.ShapeDtypeStruct((rows, block), BF16),
        ),
        in_specs=[vmem, vmem],
        out_specs=(hbm, hbm),
        scratch_shapes=[dma((2,))],
    )(out_t, out_f)
    return out_t.T[None, :, None, :], out_f[None]


def solution(mesh):
    return jax.shard_map(
        local,
        mesh=mesh,
        in_specs=(
            P("groups", "tok", "feat"),
            P("layer", "groups"),
            P("layer", "groups"),
            P("layer", None, "groups", None, None),
            P("groups"),
            P("layer", "tok", None, "feat"),
            P("layer", None, None, None, "tok", "feat"),
            P("layer", "tok", None, "feat"),
            P("layer", "feat"),
            P("layer", None, None, "tok", "feat"),
            P("layer", "groups", "tok", "feat"),
            P("layer", "feat"),
            P("layer", "feat"),
            P(),
            P("layer", "feat"),
        ),
        out_specs=(P("layer", "groups", "tok", "feat"), P("layer", "groups", "feat")),
        check_vma=False,
    )
```

```python
import functools

import jax
import jax.numpy as jnp
from jax import lax
from jax.experimental import pallas as pl
from jax.experimental.pallas import tpu as pltpu
from jax.sharding import PartitionSpec as P

F32 = jnp.float32
BF16 = jnp.bfloat16
NT = (((1,), (1,)), ((), ()))


def column(row):
    rows = row.shape[1]
    return jnp.transpose(jnp.broadcast_to(row, (128, rows)))[:, 0:1]


def kernel(
    sizes,
    lengths_in, table_in, chosen_in, attn_in, mlp_in, bias_in, mode_in, index_in,
    x_in, err_in, pat_in, wv_in, wo_in, we_in, wd_in,
    out_ref, feat_ref,
    lengths, table, chosen, scale_attn, scale_mlp, bias, mode_row, index_row,
    x_t, err_t, pat, wv, wo, we, wd,
    xbuf, slots, relay_x, nbuf, normed, masked, part_v, part_v2, vals, part_e, e_out, e_in, feats,
    acc_in, acc_out, att, err, wek, relay_in, relay_mid,
    local_sem, sent, xs_recv, zx_recv, t_recv, v_recv, m_recv, f_recv, a_recv, w_recv, b_recv,
):
    layers, feat_n, seq, prompts, head_dim, per_group, kv, width, block, rows, entries, shares = sizes
    half = seq // 2
    me_g = lax.axis_index("groups")
    me_l = lax.axis_index("layer")
    me_f = lax.axis_index("feat")
    me_t = lax.axis_index("tok")
    has_next = me_l < layers - 1
    has_prev = me_l > 0
    is_first = jnp.logical_not(has_prev)
    other = 1 - me_t
    nxt = jnp.minimum(me_l + 1, layers - 1)
    prv = jnp.maximum(me_l - 1, 0)
    streams = range(prompts)
    ends = (0, feat_n - 1)
    at_end = jnp.logical_or(me_f == 0, me_f == feat_n - 1)
    order = sorted(range(feat_n), key=lambda s: abs(2 * s - feat_n + 1))
    low_side = 2 * me_f < feat_n
    both = jnp.logical_and

    loads = [
        pltpu.make_async_copy(src, dst, local_sem.at[i])
        for i, (src, dst) in enumerate(
            (
                (x_in, x_t), (we_in, we), (attn_in, scale_attn), (lengths_in, lengths), (table_in, table),
                (chosen_in, chosen), (mlp_in, scale_mlp), (bias_in, bias), (mode_in, mode_row),
                (index_in, index_row), (wv_in, wv), (pat_in, pat), (wo_in, wo), (wd_in, wd), (err_in, err_t),
            )
        )
    ]
    for load in loads:
        load.start()
    l_x, l_we = loads[:2]

    barrier = pltpu.get_barrier_semaphore()
    mesh_id = pl.DeviceIdType.MESH

    def greet(where):
        pl.semaphore_signal(barrier, inc=1, device_id=where, device_id_type=mesh_id)

    for j in range(1, feat_n):
        for t in range(2):
            greet({"feat": (me_f + j) % feat_n, "tok": t})
    pl.when(has_next)(lambda: greet({"layer": nxt}))
    pl.when(has_prev)(lambda: greet({"layer": prv}))
    for g in range(1, shares):
        pl.when(is_first)(lambda: greet({"groups": (me_g + g) % shares, "layer": nxt}))
        pl.when(me_l == 1)(lambda: greet({"groups": (me_g + g) % shares, "layer": prv}))
    greet({"tok": other})

    def send(src, dst, rs, where):
        return pltpu.make_async_remote_copy(
            src_ref=src, dst_ref=dst, send_sem=sent.at[0], recv_sem=rs, device_id=where, device_id_type=mesh_id
        )

    def peer(j):
        return (me_f + j) % feat_n

    def far(k):
        down = feat_n - 1 - k
        return jnp.where(low_side, down - jnp.where(down <= me_f, 1, 0), k + jnp.where(k >= me_f, 1, 0))

    def part(p):
        return pl.ds(p * seq, seq)

    pending = []

    def launch(copy, cond=None):
        pending.append((copy, cond))
        if cond is None:
            copy.start()
        else:
            pl.when(cond)(copy.start)

    def landed(ref, rs):
        send(ref, ref, rs, {"tok": other}).wait_recv()

    l_x.wait()
    x_rows = jnp.transpose(x_t[...])

    @pl.when(is_first)
    def _():
        x_half = x_rows.astype(BF16)
        for p in streams:
            slots[p, me_f] = x_half[p * seq : (p + 1) * seq]
            xbuf[p] = x_rows[p * seq : (p + 1) * seq]

    extra = (shares - 1) * (1 - jnp.minimum(me_l // 2, 1))
    pl.semaphore_wait(
        barrier, 2 * feat_n - 1 + jnp.minimum(me_l, 1) + jnp.minimum(layers - 1 - me_l, 1) + extra
    )

    def share_x(p, step, cond):
        to = me_f + step
        cond = both(both(to >= 0, to < feat_n), cond)
        to = jnp.clip(to, 0, feat_n - 1)
        slot = slots.at[p, me_f]
        launch(send(slot, slot, xs_recv.at[p, me_f], {"feat": to}), cond)

    def x_landed(p, s):
        landed(slots.at[p, s], xs_recv.at[p, s])

    for p in streams:
        for step in (2, -2, 1, -1):
            share_x(p, step, is_first)

    def we_rows(s):
        return we.at[pl.ds(pl.multiple_of(s * width, 16), width)]

    l_we.wait()
    own_rows = pltpu.make_async_copy(we_rows(me_f), wek.at[me_f], local_sem.at[len(loads)])
    own_rows.start()
    share = width // shares
    my_share = me_g if shares > 1 else 0
    front = pl.ds(0, share)
    first_up = [
        send(
            we.at[pl.ds(pl.multiple_of(peer(j) * width + my_share * share, 16), share)],
            relay_in.at[peer(j), front], w_recv.at[0, peer(j)], {"layer": nxt},
        )
        for j in range(1, feat_n)
    ]
    across = [
        send(
            relay_in.at[peer(j), front], relay_mid.at[me_f, front],
            w_recv.at[1, me_f], {"feat": peer(j)},
        )
        for j in range(1, feat_n)
    ]
    back = [
        [
            send(
                relay_mid.at[peer(j), front],
                wek.at[peer(j), pl.ds(pl.multiple_of(my_share * share, 16), share)],
                b_recv.at[my_share, peer(j)],
                {"layer": prv, "groups": (me_g + g) % shares} if g else {"layer": prv},
            )
            for g in range(shares)
        ]
        for j in range(1, feat_n)
    ]
    direct = [
        send(we_rows(peer(j)), wek.at[me_f], w_recv.at[2, me_f], {"feat": peer(j)})
        for j in range(1, feat_n)
    ]

    def w_arrived(ref, stage, s):
        part_ref = ref.at[s, front] if stage < 2 else ref.at[s]
        landed(part_ref, w_recv.at[stage, s])

    @pl.when(is_first)
    def _():
        for copy in first_up:
            copy.start()

    @pl.when(me_l == 1)
    def _():
        for j in range(1, feat_n):
            w_arrived(relay_in, 0, peer(j))
            across[j - 1].start()
        for j in range(1, feat_n):
            w_arrived(relay_mid, 1, peer(j))
            for copy in back[j - 1]:
                copy.start()

    @pl.when(has_prev)
    def _():
        for copy in direct:
            copy.start()

    for load in loads[2:]:
        load.wait()
    ids = lax.broadcasted_iota(jnp.int32, (half, 1), 0) + me_t * half
    lives = [ids < lengths[p] for p in streams]
    which = jnp.zeros((1, block), jnp.int32) + chosen[0, 0]
    modes = picks = jnp.zeros((1, block), jnp.int32)
    for b in range(mode_row.shape[1] // block):
        here = which == b
        modes = jnp.where(here, mode_row[:, b * block : (b + 1) * block], modes)
        picks = jnp.where(here, index_row[:, b * block : (b + 1) * block], picks)
    levels = jnp.zeros((1, block), F32)
    for v in range(entries):
        levels = jnp.where(picks == v, table[v], levels)
    attn_col = column(scale_attn[...])
    mlp_col = column(scale_mlp[...])
    shift = bias[...]
    err[...] = jnp.transpose(err_t[...])
    q_ids = lax.broadcasted_iota(jnp.int32, (seq, seq), 0)
    k_ids = lax.broadcasted_iota(jnp.int32, (seq, seq), 1)
    for p in streams:
        keep = both(k_ids <= q_ids, k_ids < lengths[p])
        for h in range(pat.shape[0]):
            masked[h // per_group, p, pl.ds(h % per_group * seq, seq), :] = jnp.where(
                keep, pat[h, p].astype(F32), 0.0
            ).astype(BF16)
        e_in[p, 2 * me_f + me_t] = jnp.zeros((half, block), BF16)
    own_rows.wait()

    for p in streams:
        @pl.when(has_prev)
        def _():
            x_landed(p, me_f)
            xbuf[p] = slots[p, me_f].astype(F32)

        for k in range(1, feat_n):
            for step in (feat_n - k, k - feat_n):
                share_x(p, step, has_prev if abs(step) == 1 else both(has_prev, jnp.logical_not(at_end)))

    def arrival(k):
        return jnp.where(at_end, far(feat_n - 1 - k), far(k - 1)) if k else me_f

    for p in streams:
        total = jnp.zeros((seq, kv), F32)
        for k in range(feat_n):
            s = arrival(k)
            if k:
                x_landed(p, s)
                for step in (1, -1):
                    to = me_f + step
                    inside = both(to >= 0, to < feat_n)
                    relays = both(is_first, both(inside, (to - s) * step > 2))
                    to = jnp.clip(to, 0, feat_n - 1)
                    launch(send(slots.at[p, s], slots.at[p, s], xs_recv.at[p, s], {"feat": to}), relays)
            from_rows = pl.ds(pl.multiple_of(s * width, 16), width)
            total += jnp.dot(slots[p, s], wv[from_rows, :], preferred_element_type=F32)
        total *= attn_col[p * seq : (p + 1) * seq]
        part_v[p] = total.reshape(2, half, kv)
        launch(send(part_v.at[p, other], part_v2.at[p], t_recv.at[p], {"tok": other}))
        landed(part_v2.at[p], t_recv.at[p])
        vals[p, me_f, me_t] = (part_v[p, me_t] + part_v2[p]).astype(BF16)
        mine = vals.at[p, me_f, me_t]
        for k in range(feat_n - 1):
            launch(send(mine, mine, v_recv.at[p, me_f, me_t], {"feat": far(k)}))
        launch(send(mine, mine, v_recv.at[p, me_f, me_t], {"tok": other}))

    def take(p, s):
        got = vals.at[p, s, me_t]
        pl.when(me_f != s)(lambda: landed(got, v_recv.at[p, s, me_t]))
        launch(send(got, got, v_recv.at[p, s, me_t], {"tok": other}), me_f != s)

    def encode(p, cond):
        @pl.when(cond)
        def _():
            normed_mlp = normed[p]
            for k in range(feat_n):
                to = far(k) if k < feat_n - 1 else me_f
                result = jnp.dot(normed_mlp, wek[to], preferred_element_type=F32).reshape(2, half, block)
                for t in range(2):
                    e_out[p, 2 * k + t] = result[t].astype(BF16)
                if k < feat_n - 1:
                    for t in range(2):
                        e_send(p, k, t).start()
                else:
                    part_e[p] = result
                    e_swap(p).start()

    def e_send(p, k, t):
        return send(e_out.at[p, 2 * k + t], e_in.at[p, 2 * me_f + me_t], m_recv.at[p], {"feat": far(k), "tok": t})

    def e_swap(p):
        mine = 2 * (feat_n - 1) + other
        return send(e_out.at[p, mine], e_in.at[p, 2 * me_f + me_t], m_recv.at[p], {"tok": other})

    for p in streams:
        for k in range(feat_n - 1):
            for t in range(2):
                pending.append((e_send(p, k, t), None))
        pending.append((e_swap(p), None))

    for p in streams:
        total = jnp.zeros((seq, width), F32)
        for n in range(feat_n + 1):
            if n < feat_n:
                take(p, order[n])
            if n == 0:
                continue
            s = order[n - 1]
            landed(vals.at[p, s, other], v_recv.at[p, s, other])
            group = s * kv // head_dim
            d0 = s * kv % head_dim
            heads = jnp.dot(masked[group, p], vals[p, s].reshape(seq, kv), preferred_element_type=F32).astype(BF16)
            for u in range(per_group):
                total += lax.dot_general(
                    heads[u * seq : (u + 1) * seq], wo[group, u, :, pl.ds(d0, kv)], NT, preferred_element_type=F32
                )
        middle = xbuf[p] + total
        normed[p] = (middle * mlp_col[p * seq : (p + 1) * seq]).astype(BF16)
        att[part(p), :] = middle + err[part(p), :]
        if p == 0:
            for s in range(feat_n):
                pl.when(both(has_prev, me_f != s))(lambda: w_arrived(wek, 2, s))
        encode(p, has_prev)

    for s in range(feat_n):
        for g in range(shares):
            pl.when(both(is_first, me_f != s))(
                lambda: landed(wek.at[s, pl.ds(g * share, share)], b_recv.at[g, s])
            )
    for p in streams:
        encode(p, is_first)

    def await_others(ref, rs):
        landed(ref.at[pl.ds(0, 2 * feat_n - 1)], rs)

    for p in streams:
        await_others(e_in.at[p], m_recv.at[p])
        preact = part_e[p, me_t] + shift
        for s in range(2 * feat_n):
            preact += e_in[p, s].astype(F32)
        active = jnp.maximum(preact, 0.0)
        clamped = jnp.where(modes == 1, levels, jnp.where(modes == 2, active * levels, active))
        here = 2 * me_f + me_t
        feats[p, here] = jnp.where(lives[p], clamped, 0.0).astype(BF16)
        mine = feats.at[p, here]
        for k in range(feat_n - 1):
            for t in range(2):
                launch(send(mine, mine, f_recv.at[p], {"feat": far(k), "tok": t}))
        launch(send(mine, mine, f_recv.at[p], {"tok": other}))

    def features(p, s):
        return feats[p, 2 * s : 2 * s + 2].reshape(seq, block)

    def acc_copy(p, t):
        return send(acc_out.at[p, t], acc_in.at[p, t], a_recv.at[p, t], {"layer": nxt})

    for p in streams:
        @pl.when(has_prev)
        def _():
            for t in range(1, layers):
                @pl.when(t >= me_l)
                def _():
                    acc_copy(p, t).wait_recv()
            att[part(p), :] += acc_in[p, me_l]

        total = att[part(p), :]
        await_others(feats.at[p], f_recv.at[p])
        for s in range(feat_n):
            total += lax.dot_general(
                features(p, s), wd[me_l, :, pl.ds(s * block, block)], NT, preferred_element_type=F32
            )
        att[part(p), :] = total
        feat_ref[part(p), :] = feats[p, pl.ds(2 * me_f, 2)].reshape(seq, block)

        @pl.when(has_next)
        def _():
            nbuf[p] = att[part(p), :].astype(BF16)

        for k in range(feat_n - 2):
            to = jnp.where(me_f == 0, feat_n - 1 - k, k)
            launch(
                send(
                    nbuf.at[p], relay_x.at[p, jnp.minimum(me_f, 1)], zx_recv.at[p, jnp.minimum(me_f, 1)],
                    {"feat": to},
                ),
                both(has_next, at_end),
            )
        launch(send(nbuf.at[p], slots.at[p, me_f], xs_recv.at[p, me_f], {"layer": nxt}), has_next)

    for p in streams:
        for e, src in enumerate(ends):
            relays = both(has_next, jnp.abs(me_f - src) > 1)
            pl.when(relays)(lambda: landed(relay_x.at[p, e], zx_recv.at[p, e]))
            launch(send(relay_x.at[p, e], slots.at[p, src], xs_recv.at[p, src], {"layer": nxt}), relays)

    @pl.when(has_next)
    def _():
        for p in streams:
            for t in range(1, layers):
                @pl.when(t > me_l)
                def _():
                    rest = att[part(p), :] - nbuf[p].astype(F32)
                    total = jnp.where(me_l + 1 == t, rest, 0.0)
                    for s in range(feat_n):
                        total += lax.dot_general(
                            features(p, s), wd[t, :, pl.ds(s * block, block)], NT,
                            preferred_element_type=F32,
                        )
                    acc_out[p, t] = total

                    @pl.when(has_prev)
                    def _():
                        acc_out[p, t] += acc_in[p, t]

                    acc_copy(p, t).start()

    out_ref[...] = jnp.transpose(att[...])

    @pl.when(is_first)
    def _():
        for copy in first_up:
            copy.wait_send()

    @pl.when(me_l == 1)
    def _():
        for copy in sum(back, across):
            copy.wait_send()

    @pl.when(has_prev)
    def _():
        for copy in direct:
            copy.wait_send()

    for copy, cond in pending:
        if cond is None:
            copy.wait_send()
        else:
            pl.when(cond)(copy.wait_send)

    @pl.when(has_next)
    def _():
        for p in streams:
            for t in range(1, layers):
                @pl.when(t > me_l)
                def _():
                    acc_copy(p, t).wait_send()


def store(x_ref, f_ref, out_ref, feat_ref, sems):
    copies = [
        pltpu.make_async_copy(x_ref, out_ref, sems.at[0]),
        pltpu.make_async_copy(f_ref, feat_ref, sems.at[1]),
    ]
    for copy in copies:
        copy.start()
    for copy in copies:
        copy.wait()


def local(
    residual_in, attn_scale, mlp_scale, patterns, lengths, value_proj, out_proj, enc_weight, enc_bias,
    dec_weight, errors, clamp_mode, clamp_index, clamp_values, active_blocks,
):
    layers = lax.axis_size("layer")
    feat_n = lax.axis_size("feat")
    prompts, seq = patterns.shape[2], patterns.shape[3]
    head_dim, per_group = out_proj.shape[2], out_proj.shape[3]
    kv = value_proj.shape[3]
    rows, _, width = residual_in.shape
    block = enc_bias.shape[1]
    entries = clamp_values.shape[0]
    groups = lax.axis_size("groups")
    shares = groups if width % (16 * groups) == 0 else 1
    sizes = (layers, feat_n, seq, prompts, head_dim, per_group, kv, width, block, rows, entries, shares)
    x_in = residual_in[:, 0, :].T
    err_in = errors[0, :, 0, :].T
    pat_in = patterns[0]
    wv_in = value_proj[0, 0]
    wo_in = jnp.transpose(out_proj[0, :, :, :, 0, :], (0, 2, 3, 1))
    we_in = enc_weight[0, 0]
    wd_in = jnp.transpose(dec_weight[0, :, :, 0, :], (0, 2, 1))
    smem = pltpu.SMEM
    vmem = pl.BlockSpec(memory_space=pltpu.VMEM)
    hbm = pl.BlockSpec(memory_space=pl.ANY)
    small = (lengths, clamp_values, active_blocks, attn_scale, mlp_scale, enc_bias, clamp_mode, clamp_index)
    big = (x_in, err_in, pat_in, wv_in, wo_in, we_in, wd_in)
    half = seq // 2
    kv_heads = out_proj.shape[1]
    dma = pltpu.SemaphoreType.DMA
    out_t, out_f = pl.pallas_call(
        functools.partial(kernel, sizes),
        out_shape=(pltpu.VMEM((width, rows), F32), pltpu.VMEM((rows, block), BF16)),
        in_specs=[hbm] * 15,
        out_specs=(vmem, vmem),
        scratch_shapes=[(smem if i < 3 else pltpu.VMEM)(a.shape, a.dtype) for i, a in enumerate(small)]
        + [pltpu.VMEM(a.shape, a.dtype) for a in big]
        + [
            pltpu.VMEM((prompts, seq, width), F32),
            pltpu.VMEM((prompts, feat_n, seq, width), BF16),
            pltpu.VMEM((prompts, 2, seq, width), BF16),
            pltpu.VMEM((prompts, seq, width), BF16),
            pltpu.VMEM((prompts, seq, width), BF16),
            pltpu.VMEM((kv_heads, prompts, per_group * seq, seq), BF16),
            pltpu.VMEM((prompts, 2, half, kv), F32),
            pltpu.VMEM((prompts, half, kv), F32),
            pltpu.VMEM((prompts, feat_n, 2, half, kv), BF16),
            pltpu.VMEM((prompts, 2, half, block), F32),
            pltpu.VMEM((prompts, 2 * feat_n, half, block), BF16),
            pltpu.VMEM((prompts, 2 * feat_n, half, block), BF16),
            pltpu.VMEM((prompts, 2 * feat_n, half, block), BF16),
            pltpu.VMEM((prompts, layers, seq, width), F32),
            pltpu.VMEM((prompts, layers, seq, width), F32),
            pltpu.VMEM((rows, width), F32),
            pltpu.VMEM((rows, width), F32),
        ]
        + [pltpu.VMEM((feat_n, width, block), BF16)] * 3
        + [
            dma((16,)), dma((1,)), dma((prompts, feat_n)), dma((prompts, 2)), dma((prompts,)),
            dma((prompts, feat_n, 2)), dma((prompts,)), dma((prompts,)), dma((prompts, layers)),
            dma((3, feat_n)), dma((shares, feat_n)),
        ],
        compiler_params=pltpu.CompilerParams(collective_id=0, has_side_effects=True),
    )(*small, *big)
    out_t, out_f = (pltpu.with_memory_space_constraint(a, pltpu.VMEM) for a in (out_t, out_f))
    out_t, out_f = pl.pallas_call(
        store,
        out_shape=(
            jax.ShapeDtypeStruct((width, rows), F32),
            jax.ShapeDtypeStruct((rows, block), BF16),
        ),
        in_specs=[vmem, vmem],
        out_specs=(hbm, hbm),
        scratch_shapes=[dma((2,))],
    )(out_t, out_f)
    return out_t.T[None, :, None, :], out_f[None]


def solution(mesh):
    return jax.shard_map(
        local,
        mesh=mesh,
        in_specs=(
            P("groups", "tok", "feat"),
            P("layer", "groups"),
            P("layer", "groups"),
            P("layer", None, "groups", None, None),
            P("groups"),
            P("layer", "tok", None, "feat"),
            P("layer", None, None, None, "tok", "feat"),
            P("layer", "tok", None, "feat"),
            P("layer", "feat"),
            P("layer", None, None, "tok", "feat"),
            P("layer", "groups", "tok", "feat"),
            P("layer", "feat"),
            P("layer", "feat"),
            P(),
            P("layer", "feat"),
        ),
        out_specs=(P("layer", "groups", "tok", "feat"), P("layer", "groups", "feat")),
        check_vma=False,
    )
```

```python
import functools

import jax
import jax.numpy as jnp
from jax import lax
from jax.experimental import pallas as pl
from jax.experimental.pallas import tpu as pltpu
from jax.sharding import PartitionSpec as P

F32 = jnp.float32
BF16 = jnp.bfloat16
NT = (((1,), (1,)), ((), ()))


def column(row):
    rows = row.shape[1]
    return jnp.transpose(jnp.broadcast_to(row, (128, rows)))[:, 0:1]


def kernel(
    sizes,
    lengths_in, table_in, chosen_in, attn_in, mlp_in, bias_in, mode_in, index_in,
    x_in, err_in, pat_in, wv_in, wo_in, we_in, wd_in,
    out_ref, feat_ref,
    lengths, table, chosen, scale_attn, scale_mlp, bias, mode_row, index_row,
    x_t, err_t, pat, wv, wo, we, wd,
    xbuf, slots, nbuf, normed, masked, part_v, part_v2, vals, part_e, e_out, e_in, feats,
    acc_in, acc_out, att, err, wek, relay_in, relay_mid,
    local_sem, sent, up_sent, own_recv, xs_recv, t_recv, v_recv, m_recv, f_recv, a_recv, w_recv, b_recv,
):
    layers, feat_n, seq, prompts, head_dim, per_group, kv, width, block, rows, entries, shares = sizes
    half = seq // 2
    me_g = lax.axis_index("groups")
    me_l = lax.axis_index("layer")
    me_f = lax.axis_index("feat")
    me_t = lax.axis_index("tok")
    has_next = me_l < layers - 1
    has_prev = me_l > 0
    is_first = jnp.logical_not(has_prev)
    other = 1 - me_t
    nxt = jnp.minimum(me_l + 1, layers - 1)
    prv = jnp.maximum(me_l - 1, 0)
    streams = range(prompts)
    at_end = jnp.logical_or(me_f == 0, me_f == feat_n - 1)
    order = sorted(range(feat_n), key=lambda s: abs(2 * s - feat_n + 1))
    low_side = 2 * me_f < feat_n
    both = jnp.logical_and

    loads = [
        pltpu.make_async_copy(src, dst, local_sem.at[i])
        for i, (src, dst) in enumerate(
            (
                (x_in, x_t), (we_in, we), (attn_in, scale_attn), (lengths_in, lengths), (table_in, table),
                (chosen_in, chosen), (mlp_in, scale_mlp), (bias_in, bias), (mode_in, mode_row),
                (index_in, index_row), (wv_in, wv), (pat_in, pat), (wo_in, wo), (wd_in, wd), (err_in, err_t),
            )
        )
    ]
    for load in loads:
        load.start()
    l_x, l_we = loads[:2]

    barrier = pltpu.get_barrier_semaphore()
    mesh_id = pl.DeviceIdType.MESH

    def greet(where):
        pl.semaphore_signal(barrier, inc=1, device_id=where, device_id_type=mesh_id)

    for j in range(1, feat_n):
        for t in range(2):
            greet({"feat": (me_f + j) % feat_n, "tok": t})
    pl.when(has_next)(lambda: greet({"layer": nxt}))
    for s in range(feat_n):
        pl.when(both(has_prev, jnp.abs(me_f - s) != 1))(lambda: greet({"layer": prv, "feat": s}))
    for g in range(1, shares):
        pl.when(is_first)(lambda: greet({"groups": (me_g + g) % shares, "layer": nxt}))
        pl.when(me_l == 1)(lambda: greet({"groups": (me_g + g) % shares, "layer": prv}))
    greet({"tok": other})

    def send(src, dst, rs, where):
        return pltpu.make_async_remote_copy(
            src_ref=src, dst_ref=dst, send_sem=sent.at[0], recv_sem=rs, device_id=where, device_id_type=mesh_id
        )

    def peer(j):
        return (me_f + j) % feat_n

    def far(k):
        down = feat_n - 1 - k
        return jnp.where(low_side, down - jnp.where(down <= me_f, 1, 0), k + jnp.where(k >= me_f, 1, 0))

    def part(p):
        return pl.ds(p * seq, seq)

    pending = []

    def launch(copy, cond=None):
        pending.append((copy, cond))
        if cond is None:
            copy.start()
        else:
            pl.when(cond)(copy.start)

    def landed(ref, rs):
        send(ref, ref, rs, {"tok": other}).wait_recv()

    l_x.wait()
    x_rows = jnp.transpose(x_t[...])

    @pl.when(is_first)
    def _():
        x_half = x_rows.astype(BF16)
        for p in streams:
            slots[p, me_f] = x_half[p * seq : (p + 1) * seq]
            xbuf[p] = x_rows[p * seq : (p + 1) * seq]

    extra = (shares - 1) * (1 - jnp.minimum(me_l // 2, 1))
    above = jnp.minimum(layers - 1 - me_l, 1) * (feat_n - 2 + jnp.where(at_end, 1, 0))
    pl.semaphore_wait(barrier, 2 * feat_n - 1 + jnp.minimum(me_l, 1) + above + extra)

    def share_x(p, step, cond):
        to = me_f + step
        cond = both(both(to >= 0, to < feat_n), cond)
        to = jnp.clip(to, 0, feat_n - 1)
        slot = slots.at[p, me_f]
        launch(send(slot, slot, xs_recv.at[p, me_f], {"feat": to}), cond)

    def x_landed(p, s):
        landed(slots.at[p, s], xs_recv.at[p, s])

    def share_first(p):
        for step in (2, -2, 1, -1):
            share_x(p, step, is_first)

    share_first(0)

    def we_rows(s):
        return we.at[pl.ds(pl.multiple_of(s * width, 16), width)]

    l_we.wait()
    own_rows = pltpu.make_async_copy(we_rows(me_f), wek.at[me_f], local_sem.at[len(loads)])
    own_rows.start()
    share = width // shares
    my_share = me_g if shares > 1 else 0
    front = pl.ds(0, share)
    first_up = [
        send(
            we.at[pl.ds(pl.multiple_of(peer(j) * width + my_share * share, 16), share)],
            relay_in.at[peer(j), front], w_recv.at[0, peer(j)], {"layer": nxt},
        )
        for j in range(1, feat_n)
    ]
    across = [
        send(
            relay_in.at[peer(j), front], relay_mid.at[me_f, front],
            w_recv.at[1, me_f], {"feat": peer(j)},
        )
        for j in range(1, feat_n)
    ]
    back = [
        [
            send(
                relay_mid.at[peer(j), front],
                wek.at[peer(j), pl.ds(pl.multiple_of(my_share * share, 16), share)],
                b_recv.at[my_share, peer(j)],
                {"layer": prv, "groups": (me_g + g) % shares} if g else {"layer": prv},
            )
            for g in range(shares)
        ]
        for j in range(1, feat_n)
    ]
    direct = [
        send(we_rows(peer(j)), wek.at[me_f], w_recv.at[2, me_f], {"feat": peer(j)})
        for j in range(1, feat_n)
    ]

    def w_arrived(ref, stage, s):
        part_ref = ref.at[s, front] if stage < 2 else ref.at[s]
        landed(part_ref, w_recv.at[stage, s])

    def distant(j):
        return jnp.abs(peer(j) - me_f) > 1

    def next_to(j):
        return jnp.abs(peer(j) - me_f) == 1

    for j in range(1, feat_n):
        launch(first_up[j - 1], both(is_first, distant(j)))
    for j in range(1, feat_n):
        relays = both(me_l == 1, distant(j))
        pl.when(relays)(lambda: w_arrived(relay_in, 0, peer(j)))
        launch(across[j - 1], relays)
    for j in range(1, feat_n):
        relays = both(me_l == 1, distant(j))
        pl.when(relays)(lambda: w_arrived(relay_mid, 1, peer(j)))
        for copy in back[j - 1]:
            launch(copy, relays)
    for j in range(1, feat_n):
        launch(direct[j - 1], has_prev)

    for load in loads[2:]:
        load.wait()
    ids = lax.broadcasted_iota(jnp.int32, (half, 1), 0) + me_t * half
    lives = [ids < lengths[p] for p in streams]
    which = jnp.zeros((1, block), jnp.int32) + chosen[0, 0]
    modes = picks = jnp.zeros((1, block), jnp.int32)
    for b in range(mode_row.shape[1] // block):
        here = which == b
        modes = jnp.where(here, mode_row[:, b * block : (b + 1) * block], modes)
        picks = jnp.where(here, index_row[:, b * block : (b + 1) * block], picks)
    levels = jnp.zeros((1, block), F32)
    for v in range(entries):
        levels = jnp.where(picks == v, table[v], levels)
    attn_col = column(scale_attn[...])
    mlp_col = column(scale_mlp[...])
    shift = bias[...]
    err[...] = jnp.transpose(err_t[...])
    q_ids = lax.broadcasted_iota(jnp.int32, (seq, seq), 0)
    k_ids = lax.broadcasted_iota(jnp.int32, (seq, seq), 1)
    for p in streams:
        keep = both(k_ids <= q_ids, k_ids < lengths[p])
        for h in range(pat.shape[0]):
            masked[h // per_group, p, pl.ds(h % per_group * seq, seq), :] = jnp.where(
                keep, pat[h, p].astype(F32), 0.0
            ).astype(BF16)
        e_in[p, 2 * me_f + me_t] = jnp.zeros((half, block), BF16)
    own_rows.wait()

    for p in streams:
        for h in range(2):
            slot = slots.at[p, me_f, pl.ds(h * half, half)]
            pl.when(has_prev)(lambda: landed(slot, own_recv.at[p, h]))
            for step in (1, -1):
                to = me_f + step
                inside = both(has_prev, both(to >= 0, to < feat_n))
                launch(send(slot, slot, xs_recv.at[p, me_f], {"feat": jnp.clip(to, 0, feat_n - 1)}), inside)

        @pl.when(has_prev)
        def _():
            xbuf[p] = slots[p, me_f].astype(F32)

    def arrival(k):
        return jnp.where(at_end, far(feat_n - 1 - k), far(k - 1)) if k else me_f

    def v_sends(p):
        mine = vals.at[p, me_f]
        return [send(mine, mine, v_recv.at[p, me_f], {"feat": far(k)}) for k in range(feat_n - 1)]

    def v_finish(p, cond):
        @pl.when(cond)
        def _():
            landed(part_v2.at[p], t_recv.at[p])
            vals[p, me_f] = (part_v[p] + part_v2[p]).astype(BF16)
            for copy in v_sends(p):
                copy.start()

    relaying = both(is_first, jnp.logical_not(at_end))
    for p in streams:
        pending.extend((copy, None) for copy in v_sends(p))
        total = jnp.zeros((seq, kv), F32)
        if p:
            v_finish(p - 1, jnp.logical_not(relaying))
        for k in range(feat_n):
            s = arrival(k)
            if k:
                x_landed(p, s)
                for step in (1, -1):
                    to = me_f + step
                    inside = both(to >= 0, to < feat_n)
                    relays = both(is_first, both(inside, (to - s) * step > 2))
                    to = jnp.clip(to, 0, feat_n - 1)
                    launch(send(slots.at[p, s], slots.at[p, s], xs_recv.at[p, s], {"feat": to}), relays)
            if k == 1:
                if p + 1 < prompts:
                    share_first(p + 1)
                if p:
                    v_finish(p - 1, relaying)
                if p + 1 == prompts:
                    for j in range(1, feat_n):
                        launch(direct[j - 1], both(is_first, next_to(j)))
            from_rows = pl.ds(pl.multiple_of(s * width, 16), width)
            total += jnp.dot(slots[p, s], wv[from_rows, :], preferred_element_type=F32)
        total *= attn_col[p * seq : (p + 1) * seq]
        part_v[p] = total
        launch(send(part_v.at[p], part_v2.at[p], t_recv.at[p], {"tok": other}))
    v_finish(prompts - 1, me_f >= 0)

    def encode(p):
        for k in range(feat_n):
            to = far(k) if k < feat_n - 1 else me_f
            result = jnp.dot(normed[part(p), :], wek[to], preferred_element_type=F32).reshape(2, half, block)
            for t in range(2):
                e_out[p, 2 * k + t] = result[t].astype(BF16)
                if k < feat_n - 1:
                    launch(e_send(p, k, t))
            if k == feat_n - 1:
                part_e[p] = result
                launch(e_swap(p))

    def e_send(p, k, t):
        return send(e_out.at[p, 2 * k + t], e_in.at[p, 2 * me_f + me_t], m_recv.at[p], {"feat": far(k), "tok": t})

    def e_swap(p):
        mine = 2 * (feat_n - 1) + other
        return send(e_out.at[p, mine], e_in.at[p, 2 * me_f + me_t], m_recv.at[p], {"tok": other})

    for p in streams:
        total = jnp.zeros((seq, width), F32)
        for s in order:
            pl.when(me_f != s)(lambda: landed(vals.at[p, s], v_recv.at[p, s]))
            group = s * kv // head_dim
            d0 = s * kv % head_dim
            heads = jnp.dot(masked[group, p], vals[p, s], preferred_element_type=F32).astype(BF16)
            for u in range(per_group):
                total += lax.dot_general(
                    heads[u * seq : (u + 1) * seq], wo[group, u, :, pl.ds(d0, kv)], NT, preferred_element_type=F32
                )
        middle = xbuf[p] + total
        normed[part(p), :] = (middle * mlp_col[p * seq : (p + 1) * seq]).astype(BF16)
        att[part(p), :] = middle + err[part(p), :]
        if p == 0:
            for s in range(feat_n):
                apart = jnp.abs(me_f - s)
                straight = jnp.logical_or(both(has_prev, apart > 0), apart == 1)
                pl.when(straight)(lambda: w_arrived(wek, 2, s))
                for g in range(shares):
                    pl.when(both(is_first, apart > 1))(
                        lambda: landed(wek.at[s, pl.ds(g * share, share)], b_recv.at[g, s])
                    )
        encode(p)

    def await_others(ref, rs):
        landed(ref.at[pl.ds(0, 2 * feat_n - 1)], rs)

    for p in streams:
        await_others(e_in.at[p], m_recv.at[p])
        preact = part_e[p, me_t] + shift
        for s in range(2 * feat_n):
            preact += e_in[p, s].astype(F32)
        active = jnp.maximum(preact, 0.0)
        clamped = jnp.where(modes == 1, levels, jnp.where(modes == 2, active * levels, active))
        here = 2 * me_f + me_t
        feats[p, here] = jnp.where(lives[p], clamped, 0.0).astype(BF16)
        mine = feats.at[p, here]
        for k in range(feat_n - 1):
            for t in range(2):
                launch(send(mine, mine, f_recv.at[p], {"feat": far(k), "tok": t}))
        launch(send(mine, mine, f_recv.at[p], {"tok": other}))

    def features(p, s):
        return feats[p, 2 * s : 2 * s + 2].reshape(seq, block)

    def x_up(p, h):
        part_h = pl.ds(h * half, half)
        return pltpu.make_async_remote_copy(
            src_ref=nbuf.at[p, part_h], dst_ref=slots.at[p, me_f, part_h], send_sem=up_sent.at[p],
            recv_sem=own_recv.at[p, h], device_id={"layer": nxt}, device_id_type=mesh_id,
        )

    def acc_copy(p, t):
        return send(acc_out.at[p, t], acc_in.at[p, t], a_recv.at[p, t], {"layer": nxt})

    for p in streams:
        @pl.when(has_prev)
        def _():
            for t in range(1, layers):
                @pl.when(t >= me_l)
                def _():
                    acc_copy(p, t).wait_recv()
            att[part(p), :] += acc_in[p, me_l]

        total = att[part(p), :]
        await_others(feats.at[p], f_recv.at[p])
        for s in range(feat_n):
            total += lax.dot_general(
                features(p, s), wd[me_l, :, pl.ds(s * block, block)], NT, preferred_element_type=F32
            )
        att[part(p), :] = total
        feat_ref[part(p), :] = feats[p, pl.ds(2 * me_f, 2)].reshape(seq, block)

        @pl.when(has_next)
        def _():
            nbuf[p] = att[part(p), :].astype(BF16)

        for h in range(2):
            pl.when(has_next)(x_up(p, h).start)
        for k in range(feat_n - 1):
            to = far(k)
            launch(
                send(nbuf.at[p], slots.at[p, me_f], xs_recv.at[p, me_f], {"layer": nxt, "feat": to}),
                both(has_next, jnp.abs(to - me_f) > 1),
            )

    @pl.when(has_next)
    def _():
        for p in streams:
            for t in range(1, layers):
                @pl.when(t > me_l)
                def _():
                    rest = att[part(p), :] - nbuf[p].astype(F32)
                    total = jnp.where(me_l + 1 == t, rest, 0.0)
                    for s in range(feat_n):
                        total += lax.dot_general(
                            features(p, s), wd[t, :, pl.ds(s * block, block)], NT,
                            preferred_element_type=F32,
                        )
                    acc_out[p, t] = total

                    @pl.when(has_prev)
                    def _():
                        acc_out[p, t] += acc_in[p, t]

        for p in streams:
            for h in range(2):
                x_up(p, h).wait_send()
        for p in streams:
            for t in range(1, layers):
                pl.when(t > me_l)(lambda: acc_copy(p, t).start())

    out_ref[...] = jnp.transpose(att[...])

    for copy, cond in pending:
        if cond is None:
            copy.wait_send()
        else:
            pl.when(cond)(copy.wait_send)

    @pl.when(has_next)
    def _():
        for p in streams:
            for t in range(1, layers):
                @pl.when(t > me_l)
                def _():
                    acc_copy(p, t).wait_send()


def store(x_ref, f_ref, out_ref, feat_ref, sems):
    copies = [
        pltpu.make_async_copy(x_ref, out_ref, sems.at[0]),
        pltpu.make_async_copy(f_ref, feat_ref, sems.at[1]),
    ]
    for copy in copies:
        copy.start()
    for copy in copies:
        copy.wait()


def local(
    residual_in, attn_scale, mlp_scale, patterns, lengths, value_proj, out_proj, enc_weight, enc_bias,
    dec_weight, errors, clamp_mode, clamp_index, clamp_values, active_blocks,
):
    layers = lax.axis_size("layer")
    feat_n = lax.axis_size("feat")
    prompts, seq = patterns.shape[2], patterns.shape[3]
    head_dim, per_group = out_proj.shape[2], out_proj.shape[3]
    kv = value_proj.shape[3]
    rows, _, width = residual_in.shape
    block = enc_bias.shape[1]
    entries = clamp_values.shape[0]
    groups = lax.axis_size("groups")
    shares = groups if width % (16 * groups) == 0 else 1
    sizes = (layers, feat_n, seq, prompts, head_dim, per_group, kv, width, block, rows, entries, shares)
    x_in = residual_in[:, 0, :].T
    err_in = errors[0, :, 0, :].T
    pat_in = patterns[0]
    wv_in = value_proj[0, 0]
    wo_in = jnp.transpose(out_proj[0, :, :, :, 0, :], (0, 2, 3, 1))
    we_in = enc_weight[0, 0]
    wd_in = jnp.transpose(dec_weight[0, :, :, 0, :], (0, 2, 1))
    smem = pltpu.SMEM
    vmem = pl.BlockSpec(memory_space=pltpu.VMEM)
    hbm = pl.BlockSpec(memory_space=pl.ANY)
    small = (lengths, clamp_values, active_blocks, attn_scale, mlp_scale, enc_bias, clamp_mode, clamp_index)
    big = (x_in, err_in, pat_in, wv_in, wo_in, we_in, wd_in)
    half = seq // 2
    kv_heads = out_proj.shape[1]
    dma = pltpu.SemaphoreType.DMA
    out_t, out_f = pl.pallas_call(
        functools.partial(kernel, sizes),
        out_shape=(pltpu.VMEM((width, rows), F32), pltpu.VMEM((rows, block), BF16)),
        in_specs=[hbm] * 15,
        out_specs=(vmem, vmem),
        scratch_shapes=[(smem if i < 3 else pltpu.VMEM)(a.shape, a.dtype) for i, a in enumerate(small)]
        + [pltpu.VMEM(a.shape, a.dtype) for a in big]
        + [
            pltpu.VMEM((prompts, seq, width), F32),
            pltpu.VMEM((prompts, feat_n, seq, width), BF16),
            pltpu.VMEM((prompts, seq, width), BF16),
            pltpu.VMEM((rows, width), BF16),
            pltpu.VMEM((kv_heads, prompts, per_group * seq, seq), BF16),
            pltpu.VMEM((prompts, seq, kv), F32),
            pltpu.VMEM((prompts, seq, kv), F32),
            pltpu.VMEM((prompts, feat_n, seq, kv), BF16),
            pltpu.VMEM((prompts, 2, half, block), F32),
            pltpu.VMEM((prompts, 2 * feat_n, half, block), BF16),
            pltpu.VMEM((prompts, 2 * feat_n, half, block), BF16),
            pltpu.VMEM((prompts, 2 * feat_n, half, block), BF16),
            pltpu.VMEM((prompts, layers, seq, width), F32),
            pltpu.VMEM((prompts, layers, seq, width), F32),
            pltpu.VMEM((rows, width), F32),
            pltpu.VMEM((rows, width), F32),
        ]
        + [pltpu.VMEM((feat_n, width, block), BF16)] * 3
        + [
            dma((16,)), dma((1,)), dma((prompts,)), dma((prompts, 2)), dma((prompts, feat_n)), dma((prompts,)),
            dma((prompts, feat_n)), dma((prompts,)), dma((prompts,)), dma((prompts, layers)),
            dma((3, feat_n)), dma((shares, feat_n)),
        ],
        compiler_params=pltpu.CompilerParams(collective_id=0, has_side_effects=True),
    )(*small, *big)
    out_t, out_f = (pltpu.with_memory_space_constraint(a, pltpu.VMEM) for a in (out_t, out_f))
    out_t, out_f = pl.pallas_call(
        store,
        out_shape=(
            jax.ShapeDtypeStruct((width, rows), F32),
            jax.ShapeDtypeStruct((rows, block), BF16),
        ),
        in_specs=[vmem, vmem],
        out_specs=(hbm, hbm),
        scratch_shapes=[dma((2,))],
    )(out_t, out_f)
    return out_t.T[None, :, None, :], out_f[None]


def solution(mesh):
    return jax.shard_map(
        local,
        mesh=mesh,
        in_specs=(
            P("groups", "tok", "feat"),
            P("layer", "groups"),
            P("layer", "groups"),
            P("layer", None, "groups", None, None),
            P("groups"),
            P("layer", "tok", None, "feat"),
            P("layer", None, None, None, "tok", "feat"),
            P("layer", "tok", None, "feat"),
            P("layer", "feat"),
            P("layer", None, None, "tok", "feat"),
            P("layer", "groups", "tok", "feat"),
            P("layer", "feat"),
            P("layer", "feat"),
            P(),
            P("layer", "feat"),
        ),
        out_specs=(P("layer", "groups", "tok", "feat"), P("layer", "groups", "feat")),
        check_vma=False,
    )
```

```python
import functools

import jax
import jax.numpy as jnp
from jax import lax
from jax.experimental import pallas as pl
from jax.experimental.pallas import tpu as pltpu
from jax.sharding import PartitionSpec as P

F32 = jnp.float32
BF16 = jnp.bfloat16
NT = (((1,), (1,)), ((), ()))


def column(row):
    rows = row.shape[1]
    return jnp.transpose(jnp.broadcast_to(row, (128, rows)))[:, 0:1]


def kernel(
    sizes,
    lengths_in, table_in, chosen_in, attn_in, mlp_in, bias_in, mode_in, index_in,
    x_in, err_in, pat_in, wv_in, wo_in, we_in, wd_in,
    out_ref, feat_ref,
    lengths, table, chosen, scale_attn, scale_mlp, bias, mode_row, index_row,
    x_t, err_t, pat, wv, wo, we, wd,
    xbuf, slots, nbuf, normed, masked, part_v, part_v2, vals, part_e, e_out, e_in, feats,
    acc_in, acc_out, att, err, wek, relay_in, relay_mid,
    local_sem, sent, up_sent, own_recv, xs_recv, t_recv, v_recv, m_recv, f_recv, a_recv, w_recv, b_recv,
):
    layers, feat_n, seq, prompts, head_dim, per_group, kv, width, block, rows, entries, shares = sizes
    half = seq // 2
    me_g = lax.axis_index("groups")
    me_l = lax.axis_index("layer")
    me_f = lax.axis_index("feat")
    me_t = lax.axis_index("tok")
    has_next = me_l < layers - 1
    has_prev = me_l > 0
    is_first = jnp.logical_not(has_prev)
    other = 1 - me_t
    nxt = jnp.minimum(me_l + 1, layers - 1)
    prv = jnp.maximum(me_l - 1, 0)
    streams = range(prompts)
    at_end = jnp.logical_or(me_f == 0, me_f == feat_n - 1)
    order = sorted(range(feat_n), key=lambda s: abs(2 * s - feat_n + 1))
    low_side = 2 * me_f < feat_n
    both = jnp.logical_and

    loads = [
        pltpu.make_async_copy(src, dst, local_sem.at[min(i, 2)])
        for i, (src, dst) in enumerate(
            (
                (x_in, x_t), (we_in, we), (attn_in, scale_attn), (lengths_in, lengths), (table_in, table),
                (chosen_in, chosen), (mlp_in, scale_mlp), (bias_in, bias), (mode_in, mode_row),
                (index_in, index_row), (wv_in, wv), (pat_in, pat), (wo_in, wo), (wd_in, wd), (err_in, err_t),
            )
        )
    ]
    for load in loads:
        load.start()
    l_x, l_we = loads[:2]

    barrier = pltpu.get_barrier_semaphore()
    mesh_id = pl.DeviceIdType.MESH

    def greet(where):
        pl.semaphore_signal(barrier, inc=1, device_id=where, device_id_type=mesh_id)

    for j in range(1, feat_n):
        for t in range(2):
            greet({"feat": (me_f + j) % feat_n, "tok": t})
    pl.when(has_next)(lambda: greet({"layer": nxt}))
    for s in range(feat_n):
        pl.when(both(has_prev, jnp.abs(me_f - s) != 1))(lambda: greet({"layer": prv, "feat": s}))
    for g in range(1, shares):
        pl.when(is_first)(lambda: greet({"groups": (me_g + g) % shares, "layer": nxt}))
        pl.when(me_l == 1)(lambda: greet({"groups": (me_g + g) % shares, "layer": prv}))
    greet({"tok": other})

    def send(src, dst, rs, where):
        return pltpu.make_async_remote_copy(
            src_ref=src, dst_ref=dst, send_sem=sent.at[0], recv_sem=rs, device_id=where, device_id_type=mesh_id
        )

    def peer(j):
        return (me_f + j) % feat_n

    def far(k):
        down = feat_n - 1 - k
        return jnp.where(low_side, down - jnp.where(down <= me_f, 1, 0), k + jnp.where(k >= me_f, 1, 0))

    def part(p):
        return pl.ds(p * seq, seq)

    pending = []

    def launch(copy, cond=None):
        pending.append((copy, cond))
        if cond is None:
            copy.start()
        else:
            pl.when(cond)(copy.start)

    def landed(ref, rs):
        send(ref, ref, rs, {"tok": other}).wait_recv()

    l_x.wait()
    x_rows = jnp.transpose(x_t[...])

    @pl.when(is_first)
    def _():
        x_half = x_rows.astype(BF16)
        for p in streams:
            slots[p, me_f] = x_half[p * seq : (p + 1) * seq]
            xbuf[p] = x_rows[p * seq : (p + 1) * seq]

    extra = (shares - 1) * (1 - jnp.minimum(me_l // 2, 1))
    above = jnp.minimum(layers - 1 - me_l, 1) * (feat_n - 2 + jnp.where(at_end, 1, 0))
    pl.semaphore_wait(barrier, 2 * feat_n - 1 + jnp.minimum(me_l, 1) + above + extra)

    def share_x(p, step, cond):
        to = me_f + step
        cond = both(both(to >= 0, to < feat_n), cond)
        to = jnp.clip(to, 0, feat_n - 1)
        slot = slots.at[p, me_f]
        launch(send(slot, slot, xs_recv.at[p, me_f], {"feat": to}), cond)

    def x_landed(p, s):
        landed(slots.at[p, s], xs_recv.at[p, s])

    def share_first(p):
        for step in (2, -2, 1, -1):
            share_x(p, step, is_first)

    share_first(0)

    def we_rows(s):
        return we.at[pl.ds(pl.multiple_of(s * width, 16), width)]

    l_we.wait()
    own_rows = pltpu.make_async_copy(we_rows(me_f), wek.at[me_f], local_sem.at[3])
    own_rows.start()
    share = width // shares
    my_share = me_g if shares > 1 else 0
    front = pl.ds(0, share)
    first_up = [
        send(
            we.at[pl.ds(pl.multiple_of(peer(j) * width + my_share * share, 16), share)],
            relay_in.at[peer(j), front], w_recv.at[0, peer(j)], {"layer": nxt},
        )
        for j in range(1, feat_n)
    ]
    across = [
        send(
            relay_in.at[peer(j), front], relay_mid.at[me_f, front],
            w_recv.at[1, me_f], {"feat": peer(j)},
        )
        for j in range(1, feat_n)
    ]
    back = [
        [
            send(
                relay_mid.at[peer(j), front],
                wek.at[peer(j), pl.ds(pl.multiple_of(my_share * share, 16), share)],
                b_recv.at[my_share, peer(j)],
                {"layer": prv, "groups": (me_g + g) % shares} if g else {"layer": prv},
            )
            for g in range(shares)
        ]
        for j in range(1, feat_n)
    ]
    direct = [
        send(we_rows(peer(j)), wek.at[me_f], w_recv.at[2, me_f], {"feat": peer(j)})
        for j in range(1, feat_n)
    ]

    def w_arrived(ref, stage, s):
        part_ref = ref.at[s, front] if stage < 2 else ref.at[s]
        landed(part_ref, w_recv.at[stage, s])

    def distant(j):
        return jnp.abs(peer(j) - me_f) > 1

    def next_to(j):
        return jnp.abs(peer(j) - me_f) == 1

    for j in range(1, feat_n):
        launch(first_up[j - 1], both(is_first, distant(j)))
    for j in range(1, feat_n):
        relays = both(me_l == 1, distant(j))
        pl.when(relays)(lambda: w_arrived(relay_in, 0, peer(j)))
        launch(across[j - 1], relays)
    for j in range(1, feat_n):
        relays = both(me_l == 1, distant(j))
        pl.when(relays)(lambda: w_arrived(relay_mid, 1, peer(j)))
        for copy in back[j - 1]:
            launch(copy, relays)
    for j in range(1, feat_n):
        launch(direct[j - 1], has_prev)

    for load in loads[2:]:
        load.wait()
    ids = lax.broadcasted_iota(jnp.int32, (half, 1), 0) + me_t * half
    lives = [ids < lengths[p] for p in streams]
    which = jnp.zeros((1, block), jnp.int32) + chosen[0, 0]
    modes = picks = jnp.zeros((1, block), jnp.int32)
    for b in range(mode_row.shape[1] // block):
        here = which == b
        modes = jnp.where(here, mode_row[:, b * block : (b + 1) * block], modes)
        picks = jnp.where(here, index_row[:, b * block : (b + 1) * block], picks)
    levels = jnp.zeros((1, block), F32)
    for v in range(entries):
        levels = jnp.where(picks == v, table[v], levels)
    attn_col = column(scale_attn[...])
    mlp_col = column(scale_mlp[...])
    shift = bias[...]
    err[...] = jnp.transpose(err_t[...])
    q_ids = lax.broadcasted_iota(jnp.int32, (seq, seq), 0)
    k_ids = lax.broadcasted_iota(jnp.int32, (seq, seq), 1)
    for p in streams:
        keep = both(k_ids <= q_ids, k_ids < lengths[p])
        for h in range(pat.shape[0]):
            masked[h // per_group, p, pl.ds(h % per_group * seq, seq), :] = jnp.where(
                keep, pat[h, p].astype(F32), 0.0
            ).astype(BF16)
        e_in[p, 2 * me_f + me_t] = jnp.zeros((half, block), BF16)
    own_rows.wait()

    for p in streams:
        for h in range(2):
            slot = slots.at[p, me_f, pl.ds(h * half, half)]
            pl.when(has_prev)(lambda: landed(slot, own_recv.at[p, h]))
            for step in (1, -1):
                to = me_f + step
                inside = both(has_prev, both(to >= 0, to < feat_n))
                launch(send(slot, slot, xs_recv.at[p, me_f], {"feat": jnp.clip(to, 0, feat_n - 1)}), inside)

        @pl.when(has_prev)
        def _():
            xbuf[p] = slots[p, me_f].astype(F32)

    def arrival(k):
        return jnp.where(at_end, far(feat_n - 1 - k), far(k - 1)) if k else me_f

    def v_sends(p):
        mine = vals.at[p, me_f]
        return [send(mine, mine, v_recv.at[p, me_f], {"feat": far(k)}) for k in range(feat_n - 1)]

    def v_finish(p, cond):
        @pl.when(cond)
        def _():
            landed(part_v2.at[p], t_recv.at[p])
            vals[p, me_f] = (part_v[p] + part_v2[p]).astype(BF16)
            for copy in v_sends(p):
                copy.start()

    relaying = both(is_first, jnp.logical_not(at_end))
    for p in streams:
        pending.extend((copy, None) for copy in v_sends(p))
        total = jnp.zeros((seq, kv), F32)
        if p:
            v_finish(p - 1, jnp.logical_not(relaying))
        for k in range(feat_n):
            s = arrival(k)
            if k:
                x_landed(p, s)
                for step in (1, -1):
                    to = me_f + step
                    inside = both(to >= 0, to < feat_n)
                    relays = both(is_first, both(inside, (to - s) * step > 2))
                    to = jnp.clip(to, 0, feat_n - 1)
                    launch(send(slots.at[p, s], slots.at[p, s], xs_recv.at[p, s], {"feat": to}), relays)
            if k == 1:
                if p + 1 < prompts:
                    share_first(p + 1)
                if p:
                    v_finish(p - 1, relaying)
                if p + 1 == prompts:
                    for j in range(1, feat_n):
                        launch(direct[j - 1], both(is_first, next_to(j)))
            from_rows = pl.ds(pl.multiple_of(s * width, 16), width)
            total += jnp.dot(slots[p, s], wv[from_rows, :], preferred_element_type=F32)
        total *= attn_col[p * seq : (p + 1) * seq]
        part_v[p] = total
        launch(send(part_v.at[p], part_v2.at[p], t_recv.at[p], {"tok": other}))
    v_finish(prompts - 1, me_f >= 0)

    def encode(p):
        for k in range(feat_n):
            to = far(k) if k < feat_n - 1 else me_f
            result = jnp.dot(normed[part(p), :], wek[to], preferred_element_type=F32).reshape(2, half, block)
            for t in range(2):
                e_out[p, 2 * k + t] = result[t].astype(BF16)
                if k < feat_n - 1:
                    launch(e_send(p, k, t))
            if k == feat_n - 1:
                part_e[p] = result
                launch(e_swap(p))

    def e_send(p, k, t):
        return send(e_out.at[p, 2 * k + t], e_in.at[p, 2 * me_f + me_t], m_recv.at[p], {"feat": far(k), "tok": t})

    def e_swap(p):
        mine = 2 * (feat_n - 1) + other
        return send(e_out.at[p, mine], e_in.at[p, 2 * me_f + me_t], m_recv.at[p], {"tok": other})

    for p in streams:
        total = jnp.zeros((seq, width), F32)
        for s in order:
            pl.when(me_f != s)(lambda: landed(vals.at[p, s], v_recv.at[p, s]))
            group = s * kv // head_dim
            d0 = s * kv % head_dim
            heads = jnp.dot(masked[group, p], vals[p, s], preferred_element_type=F32).astype(BF16)
            for u in range(per_group):
                total += lax.dot_general(
                    heads[u * seq : (u + 1) * seq], wo[group, u, :, pl.ds(d0, kv)], NT, preferred_element_type=F32
                )
        middle = xbuf[p] + total
        normed[part(p), :] = (middle * mlp_col[p * seq : (p + 1) * seq]).astype(BF16)
        att[part(p), :] = middle + err[part(p), :]
        if p == 0:
            for s in range(feat_n):
                apart = jnp.abs(me_f - s)
                straight = jnp.logical_or(both(has_prev, apart > 0), apart == 1)
                pl.when(straight)(lambda: w_arrived(wek, 2, s))
                for g in range(shares):
                    pl.when(both(is_first, apart > 1))(
                        lambda: landed(wek.at[s, pl.ds(g * share, share)], b_recv.at[g, s])
                    )
        encode(p)

    def await_others(ref, rs):
        landed(ref.at[pl.ds(0, 2 * feat_n - 1)], rs)

    for p in streams:
        await_others(e_in.at[p], m_recv.at[p])
        preact = part_e[p, me_t] + shift
        for s in range(2 * feat_n):
            preact += e_in[p, s].astype(F32)
        active = jnp.maximum(preact, 0.0)
        clamped = jnp.where(modes == 1, levels, jnp.where(modes == 2, active * levels, active))
        here = 2 * me_f + me_t
        feats[p, here] = jnp.where(lives[p], clamped, 0.0).astype(BF16)
        mine = feats.at[p, here]
        for k in range(feat_n - 1):
            for t in range(2):
                launch(send(mine, mine, f_recv.at[p], {"feat": far(k), "tok": t}))
        launch(send(mine, mine, f_recv.at[p], {"tok": other}))

    pair = 2 if feat_n % 2 == 0 else 1

    def decode(p, t, total):
        for s in range(0, feat_n, pair):
            lhs = [feats[p, 2 * i : 2 * i + 2].reshape(seq, block) for i in range(s, s + pair)]
            total += lax.dot_general(
                jnp.concatenate(lhs, axis=1), wd[t, :, pl.ds(s * block, pair * block)], NT,
                preferred_element_type=F32,
            )
        return total

    def x_up(p, h):
        part_h = pl.ds(h * half, half)
        return pltpu.make_async_remote_copy(
            src_ref=nbuf.at[p, part_h], dst_ref=slots.at[p, me_f, part_h], send_sem=up_sent.at[p],
            recv_sem=own_recv.at[p, h], device_id={"layer": nxt}, device_id_type=mesh_id,
        )

    def acc_copy(p, t):
        return send(acc_out.at[p, t], acc_in.at[p, t], a_recv.at[p, t - 1], {"layer": nxt})

    for p in streams:
        @pl.when(has_prev)
        def _():
            for t in range(1, layers):
                @pl.when(t >= me_l)
                def _():
                    acc_copy(p, t).wait_recv()
            att[part(p), :] += acc_in[p, me_l]

        total = att[part(p), :]
        await_others(feats.at[p], f_recv.at[p])
        att[part(p), :] = decode(p, me_l, total)
        feat_ref[part(p), :] = feats[p, pl.ds(2 * me_f, 2)].reshape(seq, block)

        @pl.when(has_next)
        def _():
            nbuf[p] = att[part(p), :].astype(BF16)

        for h in range(2):
            pl.when(has_next)(x_up(p, h).start)
        for k in range(feat_n - 1):
            to = far(k)
            launch(
                send(nbuf.at[p], slots.at[p, me_f], xs_recv.at[p, me_f], {"layer": nxt, "feat": to}),
                both(has_next, jnp.abs(to - me_f) > 1),
            )

    @pl.when(has_next)
    def _():
        for p in streams:
            for t in range(1, layers):
                @pl.when(t > me_l)
                def _():
                    rest = att[part(p), :] - nbuf[p].astype(F32)
                    total = jnp.where(me_l + 1 == t, rest, 0.0)
                    acc_out[p, t] = decode(p, t, total)

                    @pl.when(has_prev)
                    def _():
                        acc_out[p, t] += acc_in[p, t]

        for p in streams:
            for h in range(2):
                x_up(p, h).wait_send()
        for p in streams:
            for t in range(1, layers):
                pl.when(t > me_l)(lambda: acc_copy(p, t).start())

    out_ref[...] = jnp.transpose(att[...])

    for copy, cond in pending:
        if cond is None:
            copy.wait_send()
        else:
            pl.when(cond)(copy.wait_send)

    @pl.when(has_next)
    def _():
        for p in streams:
            for t in range(1, layers):
                @pl.when(t > me_l)
                def _():
                    acc_copy(p, t).wait_send()


def store(x_ref, f_ref, out_ref, feat_ref, sems):
    copies = [
        pltpu.make_async_copy(x_ref, out_ref, sems.at[0]),
        pltpu.make_async_copy(f_ref, feat_ref, sems.at[1]),
    ]
    for copy in copies:
        copy.start()
    for copy in copies:
        copy.wait()


def local(
    residual_in, attn_scale, mlp_scale, patterns, lengths, value_proj, out_proj, enc_weight, enc_bias,
    dec_weight, errors, clamp_mode, clamp_index, clamp_values, active_blocks,
):
    layers = lax.axis_size("layer")
    feat_n = lax.axis_size("feat")
    prompts, seq = patterns.shape[2], patterns.shape[3]
    head_dim, per_group = out_proj.shape[2], out_proj.shape[3]
    kv = value_proj.shape[3]
    rows, _, width = residual_in.shape
    block = enc_bias.shape[1]
    entries = clamp_values.shape[0]
    groups = lax.axis_size("groups")
    shares = groups if width % (16 * groups) == 0 else 1
    sizes = (layers, feat_n, seq, prompts, head_dim, per_group, kv, width, block, rows, entries, shares)
    x_in = residual_in[:, 0, :].T
    err_in = errors[0, :, 0, :].T
    pat_in = patterns[0]
    wv_in = value_proj[0, 0]
    wo_in = jnp.transpose(out_proj[0, :, :, :, 0, :], (0, 2, 3, 1))
    we_in = enc_weight[0, 0]
    wd_in = jnp.transpose(dec_weight[0, :, :, 0, :], (0, 2, 1))
    smem = pltpu.SMEM
    vmem = pl.BlockSpec(memory_space=pltpu.VMEM)
    hbm = pl.BlockSpec(memory_space=pl.ANY)
    small = (lengths, clamp_values, active_blocks, attn_scale, mlp_scale, enc_bias, clamp_mode, clamp_index)
    big = (x_in, err_in, pat_in, wv_in, wo_in, we_in, wd_in)
    half = seq // 2
    kv_heads = out_proj.shape[1]
    dma = pltpu.SemaphoreType.DMA
    out_t, out_f = pl.pallas_call(
        functools.partial(kernel, sizes),
        out_shape=(pltpu.VMEM((width, rows), F32), pltpu.VMEM((rows, block), BF16)),
        in_specs=[hbm] * 15,
        out_specs=(vmem, vmem),
        scratch_shapes=[(smem if i < 3 else pltpu.VMEM)(a.shape, a.dtype) for i, a in enumerate(small)]
        + [pltpu.VMEM(a.shape, a.dtype) for a in big]
        + [
            pltpu.VMEM((prompts, seq, width), F32),
            pltpu.VMEM((prompts, feat_n, seq, width), BF16),
            pltpu.VMEM((prompts, seq, width), BF16),
            pltpu.VMEM((rows, width), BF16),
            pltpu.VMEM((kv_heads, prompts, per_group * seq, seq), BF16),
            pltpu.VMEM((prompts, seq, kv), F32),
            pltpu.VMEM((prompts, seq, kv), F32),
            pltpu.VMEM((prompts, feat_n, seq, kv), BF16),
            pltpu.VMEM((prompts, 2, half, block), F32),
            pltpu.VMEM((prompts, 2 * feat_n, half, block), BF16),
            pltpu.VMEM((prompts, 2 * feat_n, half, block), BF16),
            pltpu.VMEM((prompts, 2 * feat_n, half, block), BF16),
            pltpu.VMEM((prompts, layers, seq, width), F32),
            pltpu.VMEM((prompts, layers, seq, width), F32),
            pltpu.VMEM((rows, width), F32),
            pltpu.VMEM((rows, width), F32),
        ]
        + [pltpu.VMEM((feat_n, width, block), BF16)] * 3
        + [
            dma((4,)), dma((1,)), dma((prompts,)), dma((prompts, 2)), dma((prompts, feat_n)), dma((prompts,)),
            dma((prompts, feat_n)), dma((prompts,)), dma((prompts,)), dma((prompts, layers - 1)),
            dma((3, feat_n)), dma((shares, feat_n)),
        ],
        compiler_params=pltpu.CompilerParams(collective_id=0, has_side_effects=True),
    )(*small, *big)
    out_t, out_f = (pltpu.with_memory_space_constraint(a, pltpu.VMEM) for a in (out_t, out_f))
    out_t, out_f = pl.pallas_call(
        store,
        out_shape=(
            jax.ShapeDtypeStruct((width, rows), F32),
            jax.ShapeDtypeStruct((rows, block), BF16),
        ),
        in_specs=[vmem, vmem],
        out_specs=(hbm, hbm),
        scratch_shapes=[dma((2,))],
    )(out_t, out_f)
    return out_t.T[None, :, None, :], out_f[None]


def solution(mesh):
    return jax.shard_map(
        local,
        mesh=mesh,
        in_specs=(
            P("groups", "tok", "feat"),
            P("layer", "groups"),
            P("layer", "groups"),
            P("layer", None, "groups", None, None),
            P("groups"),
            P("layer", "tok", None, "feat"),
            P("layer", None, None, None, "tok", "feat"),
            P("layer", "tok", None, "feat"),
            P("layer", "feat"),
            P("layer", None, None, "tok", "feat"),
            P("layer", "groups", "tok", "feat"),
            P("layer", "feat"),
            P("layer", "feat"),
            P(),
            P("layer", "feat"),
        ),
        out_specs=(P("layer", "groups", "tok", "feat"), P("layer", "groups", "feat")),
        check_vma=False,
    )
```

```python
import functools

import jax
import jax.numpy as jnp
from jax import lax
from jax.experimental import pallas as pl
from jax.experimental.pallas import tpu as pltpu
from jax.sharding import PartitionSpec as P

F32 = jnp.float32
BF16 = jnp.bfloat16
NT = (((1,), (1,)), ((), ()))


def column(row):
    rows = row.shape[1]
    return jnp.transpose(jnp.broadcast_to(row, (128, rows)))[:, 0:1]


def kernel(
    sizes,
    lengths_in, table_in, chosen_in, attn_in, mlp_in, bias_in, mode_in, index_in,
    x_in, err_in, pat_in, wv_in, wo_in, we_in, wd_in,
    out_ref, feat_ref,
    lengths, table, chosen, scale_attn, scale_mlp, bias, mode_row, index_row,
    x_t, err_t, pat, wv, wo, we, wd,
    xbuf, slots, nbuf, normed, masked, part_v, part_v2, vals, part_e, e_out, e_in, feats,
    acc_in, acc_out, att, err, wek, relay_in, relay_mid,
    local_sem, ready, sent, up_sent, own_recv, xs_recv, t_recv, v_recv, m_recv, f_recv, a_recv, w_recv, b_recv,
):
    layers, feat_n, seq, prompts, head_dim, per_group, kv, width, block, rows, entries, shares = sizes
    half = seq // 2
    me_g = lax.axis_index("groups")
    me_l = lax.axis_index("layer")
    me_f = lax.axis_index("feat")
    me_t = lax.axis_index("tok")
    has_next = me_l < layers - 1
    has_prev = me_l > 0
    is_first = jnp.logical_not(has_prev)
    other = 1 - me_t
    nxt = jnp.minimum(me_l + 1, layers - 1)
    prv = jnp.maximum(me_l - 1, 0)
    streams = range(prompts)
    at_end = jnp.logical_or(me_f == 0, me_f == feat_n - 1)
    order = sorted(range(feat_n), key=lambda s: abs(2 * s - feat_n + 1))
    low_side = 2 * me_f < feat_n
    both = jnp.logical_and

    loads = [
        pltpu.make_async_copy(src, dst, local_sem.at[min(i, 2)])
        for i, (src, dst) in enumerate(
            (
                (x_in, x_t), (we_in, we), (attn_in, scale_attn), (lengths_in, lengths), (table_in, table),
                (chosen_in, chosen), (mlp_in, scale_mlp), (bias_in, bias), (mode_in, mode_row),
                (index_in, index_row), (wv_in, wv), (pat_in, pat), (wo_in, wo), (wd_in, wd), (err_in, err_t),
            )
        )
    ]
    for load in loads:
        load.start()
    l_x, l_we = loads[:2]

    barrier = pltpu.get_barrier_semaphore()
    mesh_id = pl.DeviceIdType.MESH

    def greet(where):
        pl.semaphore_signal(barrier, inc=1, device_id=where, device_id_type=mesh_id)

    for j in range(1, feat_n):
        for t in range(2):
            greet({"feat": (me_f + j) % feat_n, "tok": t})
    for s in range(feat_n):
        pl.when(both(has_next, jnp.abs(me_f - s) != 1))(lambda: greet({"layer": nxt, "feat": s}))
    for g in range(1, shares):
        pl.when(is_first)(lambda: greet({"groups": (me_g + g) % shares, "layer": nxt}))
    greet({"tok": other})

    def send(src, dst, rs, where):
        return pltpu.make_async_remote_copy(
            src_ref=src, dst_ref=dst, send_sem=sent.at[0], recv_sem=rs, device_id=where, device_id_type=mesh_id
        )

    def peer(j):
        return (me_f + j) % feat_n

    def far(k):
        down = feat_n - 1 - k
        return jnp.where(low_side, down - jnp.where(down <= me_f, 1, 0), k + jnp.where(k >= me_f, 1, 0))

    def part(p):
        return pl.ds(p * seq, seq)

    pending = []

    def launch(copy, cond=None):
        pending.append((copy, cond))
        if cond is None:
            copy.start()
        else:
            pl.when(cond)(copy.start)

    def landed(ref, rs):
        send(ref, ref, rs, {"tok": other}).wait_recv()

    l_x.wait()
    x_rows = jnp.transpose(x_t[...])

    @pl.when(is_first)
    def _():
        x_half = x_rows.astype(BF16)
        for p in streams:
            slots[p, me_f] = x_half[p * seq : (p + 1) * seq]
            xbuf[p] = x_rows[p * seq : (p + 1) * seq]

    met = feat_n - 2 + jnp.where(at_end, 1, 0)
    second = jnp.minimum(me_l, 1) * (1 - jnp.minimum(me_l // 2, 1))
    pl.semaphore_wait(barrier, 2 * feat_n - 1 + jnp.minimum(me_l, 1) * met + second * (shares - 1))
    for s in range(feat_n):
        @pl.when(both(has_prev, jnp.abs(me_f - s) != 1))
        def _():
            slot = jnp.minimum(jnp.abs(me_f - s), 1)
            pl.semaphore_signal(ready.at[slot], inc=1, device_id={"layer": prv, "feat": s}, device_id_type=mesh_id)

    def share_x(p, step, cond):
        to = me_f + step
        cond = both(both(to >= 0, to < feat_n), cond)
        to = jnp.clip(to, 0, feat_n - 1)
        slot = slots.at[p, me_f]
        launch(send(slot, slot, xs_recv.at[p, me_f], {"feat": to}), cond)

    def x_landed(p, s):
        landed(slots.at[p, s], xs_recv.at[p, s])

    def share_first(p):
        for step in (2, -2, 1, -1):
            share_x(p, step, is_first)

    share_first(0)

    def we_rows(s):
        return we.at[pl.ds(pl.multiple_of(s * width, 16), width)]

    l_we.wait()
    own_rows = pltpu.make_async_copy(we_rows(me_f), wek.at[me_f], local_sem.at[3])
    own_rows.start()
    share = width // shares
    my_share = me_g if shares > 1 else 0
    front = pl.ds(0, share)
    first_up = [
        send(
            we.at[pl.ds(pl.multiple_of(peer(j) * width + my_share * share, 16), share)],
            relay_in.at[peer(j), front], w_recv.at[0, peer(j)], {"layer": nxt},
        )
        for j in range(1, feat_n)
    ]
    across = [
        send(
            relay_in.at[peer(j), front], relay_mid.at[me_f, front],
            w_recv.at[1, me_f], {"feat": peer(j)},
        )
        for j in range(1, feat_n)
    ]
    back = [
        [
            send(
                relay_mid.at[peer(j), front],
                wek.at[peer(j), pl.ds(pl.multiple_of(my_share * share, 16), share)],
                b_recv.at[my_share, peer(j)],
                {"layer": prv, "groups": (me_g + g) % shares} if g else {"layer": prv},
            )
            for g in range(shares)
        ]
        for j in range(1, feat_n)
    ]
    direct = [
        send(we_rows(peer(j)), wek.at[me_f], w_recv.at[2, me_f], {"feat": peer(j)})
        for j in range(1, feat_n)
    ]

    def w_arrived(ref, stage, s):
        part_ref = ref.at[s, front] if stage < 2 else ref.at[s]
        landed(part_ref, w_recv.at[stage, s])

    def distant(j):
        return jnp.abs(peer(j) - me_f) > 1

    def next_to(j):
        return jnp.abs(peer(j) - me_f) == 1

    pl.when(has_next)(lambda: pl.semaphore_wait(ready.at[0], 1))
    for j in range(1, feat_n):
        launch(first_up[j - 1], both(is_first, distant(j)))
    for j in range(1, feat_n):
        relays = both(me_l == 1, distant(j))
        pl.when(relays)(lambda: w_arrived(relay_in, 0, peer(j)))
        launch(across[j - 1], relays)
    for j in range(1, feat_n):
        relays = both(me_l == 1, distant(j))
        pl.when(relays)(lambda: w_arrived(relay_mid, 1, peer(j)))
        for copy in back[j - 1]:
            launch(copy, relays)
    for j in range(1, feat_n):
        launch(direct[j - 1], has_prev)

    for load in loads[2:]:
        load.wait()
    ids = lax.broadcasted_iota(jnp.int32, (half, 1), 0) + me_t * half
    lives = [ids < lengths[p] for p in streams]
    which = jnp.zeros((1, block), jnp.int32) + chosen[0, 0]
    modes = picks = jnp.zeros((1, block), jnp.int32)
    for b in range(mode_row.shape[1] // block):
        here = which == b
        modes = jnp.where(here, mode_row[:, b * block : (b + 1) * block], modes)
        picks = jnp.where(here, index_row[:, b * block : (b + 1) * block], picks)
    levels = jnp.zeros((1, block), F32)
    for v in range(entries):
        levels = jnp.where(picks == v, table[v], levels)
    attn_col = column(scale_attn[...])
    mlp_col = column(scale_mlp[...])
    shift = bias[...]
    err[...] = jnp.transpose(err_t[...])
    q_ids = lax.broadcasted_iota(jnp.int32, (seq, seq), 0)
    k_ids = lax.broadcasted_iota(jnp.int32, (seq, seq), 1)
    for p in streams:
        keep = both(k_ids <= q_ids, k_ids < lengths[p])
        for h in range(pat.shape[0]):
            masked[h // per_group, p, pl.ds(h % per_group * seq, seq), :] = jnp.where(
                keep, pat[h, p].astype(F32), 0.0
            ).astype(BF16)
        e_in[p, 2 * me_f + me_t] = jnp.zeros((half, block), BF16)
    own_rows.wait()

    for p in streams:
        for h in range(2):
            slot = slots.at[p, me_f, pl.ds(h * half, half)]
            pl.when(has_prev)(lambda: landed(slot, own_recv.at[p, h]))
            for step in (1, -1):
                to = me_f + step
                inside = both(has_prev, both(to >= 0, to < feat_n))
                launch(send(slot, slot, xs_recv.at[p, me_f], {"feat": jnp.clip(to, 0, feat_n - 1)}), inside)

        @pl.when(has_prev)
        def _():
            xbuf[p] = slots[p, me_f].astype(F32)

    def arrival(k):
        return jnp.where(at_end, far(feat_n - 1 - k), far(k - 1)) if k else me_f

    def v_sends(p):
        mine = vals.at[p, me_f]
        return [send(mine, mine, v_recv.at[p, me_f], {"feat": far(k)}) for k in range(feat_n - 1)]

    def v_finish(p, cond):
        @pl.when(cond)
        def _():
            landed(part_v2.at[p], t_recv.at[p])
            vals[p, me_f] = (part_v[p] + part_v2[p]).astype(BF16)
            for copy in v_sends(p):
                copy.start()

    relaying = both(is_first, jnp.logical_not(at_end))
    for p in streams:
        pending.extend((copy, None) for copy in v_sends(p))
        total = jnp.zeros((seq, kv), F32)
        if p:
            v_finish(p - 1, jnp.logical_not(relaying))
        for k in range(feat_n):
            s = arrival(k)
            if k:
                x_landed(p, s)
                for step in (1, -1):
                    to = me_f + step
                    inside = both(to >= 0, to < feat_n)
                    relays = both(is_first, both(inside, (to - s) * step > 2))
                    to = jnp.clip(to, 0, feat_n - 1)
                    launch(send(slots.at[p, s], slots.at[p, s], xs_recv.at[p, s], {"feat": to}), relays)
            if k == 1:
                if p + 1 < prompts:
                    share_first(p + 1)
                if p:
                    v_finish(p - 1, relaying)
                if p + 1 == prompts:
                    for j in range(1, feat_n):
                        launch(direct[j - 1], both(is_first, next_to(j)))
            from_rows = pl.ds(pl.multiple_of(s * width, 16), width)
            total += jnp.dot(slots[p, s], wv[from_rows, :], preferred_element_type=F32)
        total *= attn_col[p * seq : (p + 1) * seq]
        part_v[p] = total
        launch(send(part_v.at[p], part_v2.at[p], t_recv.at[p], {"tok": other}))
    v_finish(prompts - 1, me_f >= 0)

    def encode(p):
        for k in range(feat_n):
            to = far(k) if k < feat_n - 1 else me_f
            result = jnp.dot(normed[part(p), :], wek[to], preferred_element_type=F32).reshape(2, half, block)
            for t in range(2):
                e_out[p, 2 * k + t] = result[t].astype(BF16)
                if k < feat_n - 1:
                    launch(e_send(p, k, t))
            if k == feat_n - 1:
                part_e[p] = result
                launch(e_swap(p))

    def e_send(p, k, t):
        return send(e_out.at[p, 2 * k + t], e_in.at[p, 2 * me_f + me_t], m_recv.at[p], {"feat": far(k), "tok": t})

    def e_swap(p):
        mine = 2 * (feat_n - 1) + other
        return send(e_out.at[p, mine], e_in.at[p, 2 * me_f + me_t], m_recv.at[p], {"tok": other})

    for p in streams:
        total = jnp.zeros((seq, width), F32)
        for s in order:
            pl.when(me_f != s)(lambda: landed(vals.at[p, s], v_recv.at[p, s]))
            group = s * kv // head_dim
            d0 = s * kv % head_dim
            heads = jnp.dot(masked[group, p], vals[p, s], preferred_element_type=F32).astype(BF16)
            for u in range(per_group):
                total += lax.dot_general(
                    heads[u * seq : (u + 1) * seq], wo[group, u, :, pl.ds(d0, kv)], NT, preferred_element_type=F32
                )
        middle = xbuf[p] + total
        normed[part(p), :] = (middle * mlp_col[p * seq : (p + 1) * seq]).astype(BF16)
        att[part(p), :] = middle + err[part(p), :]
        if p == 0:
            for s in range(feat_n):
                apart = jnp.abs(me_f - s)
                straight = jnp.logical_or(both(has_prev, apart > 0), apart == 1)
                pl.when(straight)(lambda: w_arrived(wek, 2, s))
                for g in range(shares):
                    pl.when(both(is_first, apart > 1))(
                        lambda: landed(wek.at[s, pl.ds(g * share, share)], b_recv.at[g, s])
                    )
        encode(p)

    def await_others(ref, rs):
        landed(ref.at[pl.ds(0, 2 * feat_n - 1)], rs)

    for p in streams:
        await_others(e_in.at[p], m_recv.at[p])
        preact = part_e[p, me_t] + shift
        for s in range(2 * feat_n):
            preact += e_in[p, s].astype(F32)
        active = jnp.maximum(preact, 0.0)
        clamped = jnp.where(modes == 1, levels, jnp.where(modes == 2, active * levels, active))
        here = 2 * me_f + me_t
        feats[p, here] = jnp.where(lives[p], clamped, 0.0).astype(BF16)
        mine = feats.at[p, here]
        for k in range(feat_n - 1):
            for t in range(2):
                launch(send(mine, mine, f_recv.at[p], {"feat": far(k), "tok": t}))
        launch(send(mine, mine, f_recv.at[p], {"tok": other}))

    pair = 2 if feat_n % 2 == 0 else 1

    def decode(p, t, total):
        for s in range(0, feat_n, pair):
            lhs = [feats[p, 2 * i : 2 * i + 2].reshape(seq, block) for i in range(s, s + pair)]
            total += lax.dot_general(
                jnp.concatenate(lhs, axis=1), wd[t, :, pl.ds(s * block, pair * block)], NT,
                preferred_element_type=F32,
            )
        return total

    def x_up(p, h):
        part_h = pl.ds(h * half, half)
        return pltpu.make_async_remote_copy(
            src_ref=nbuf.at[p, part_h], dst_ref=slots.at[p, me_f, part_h], send_sem=up_sent.at[p],
            recv_sem=own_recv.at[p, h], device_id={"layer": nxt}, device_id_type=mesh_id,
        )

    def acc_copy(p, t):
        return send(acc_out.at[p, t], acc_in.at[p, t], a_recv.at[p, t - 1], {"layer": nxt})

    pl.when(has_next)(lambda: pl.semaphore_wait(ready.at[1], met - 1))
    for p in streams:
        @pl.when(has_prev)
        def _():
            for t in range(1, layers):
                @pl.when(t >= me_l)
                def _():
                    acc_copy(p, t).wait_recv()
            att[part(p), :] += acc_in[p, me_l]

        total = att[part(p), :]
        await_others(feats.at[p], f_recv.at[p])
        att[part(p), :] = decode(p, me_l, total)
        feat_ref[part(p), :] = feats[p, pl.ds(2 * me_f, 2)].reshape(seq, block)

        @pl.when(has_next)
        def _():
            nbuf[p] = att[part(p), :].astype(BF16)

        for h in range(2):
            pl.when(has_next)(x_up(p, h).start)
        for k in range(feat_n - 1):
            to = far(k)
            launch(
                send(nbuf.at[p], slots.at[p, me_f], xs_recv.at[p, me_f], {"layer": nxt, "feat": to}),
                both(has_next, jnp.abs(to - me_f) > 1),
            )

    @pl.when(has_next)
    def _():
        for p in streams:
            for t in range(1, layers):
                @pl.when(t > me_l)
                def _():
                    rest = att[part(p), :] - nbuf[p].astype(F32)
                    total = jnp.where(me_l + 1 == t, rest, 0.0)
                    acc_out[p, t] = decode(p, t, total)

                    @pl.when(has_prev)
                    def _():
                        acc_out[p, t] += acc_in[p, t]

        for p in streams:
            for h in range(2):
                x_up(p, h).wait_send()
        for p in streams:
            for t in range(1, layers):
                pl.when(t > me_l)(lambda: acc_copy(p, t).start())

    out_ref[...] = jnp.transpose(att[...])

    for copy, cond in pending:
        if cond is None:
            copy.wait_send()
        else:
            pl.when(cond)(copy.wait_send)

    @pl.when(has_next)
    def _():
        for p in streams:
            for t in range(1, layers):
                @pl.when(t > me_l)
                def _():
                    acc_copy(p, t).wait_send()


def store(x_ref, f_ref, out_ref, feat_ref, sems):
    copies = [
        pltpu.make_async_copy(x_ref, out_ref, sems.at[0]),
        pltpu.make_async_copy(f_ref, feat_ref, sems.at[1]),
    ]
    for copy in copies:
        copy.start()
    for copy in copies:
        copy.wait()


def local(
    residual_in, attn_scale, mlp_scale, patterns, lengths, value_proj, out_proj, enc_weight, enc_bias,
    dec_weight, errors, clamp_mode, clamp_index, clamp_values, active_blocks,
):
    layers = lax.axis_size("layer")
    feat_n = lax.axis_size("feat")
    prompts, seq = patterns.shape[2], patterns.shape[3]
    head_dim, per_group = out_proj.shape[2], out_proj.shape[3]
    kv = value_proj.shape[3]
    rows, _, width = residual_in.shape
    block = enc_bias.shape[1]
    entries = clamp_values.shape[0]
    groups = lax.axis_size("groups")
    shares = groups if width % (16 * groups) == 0 else 1
    sizes = (layers, feat_n, seq, prompts, head_dim, per_group, kv, width, block, rows, entries, shares)
    x_in = residual_in[:, 0, :].T
    err_in = errors[0, :, 0, :].T
    pat_in = patterns[0]
    wv_in = value_proj[0, 0]
    wo_in = jnp.transpose(out_proj[0, :, :, :, 0, :], (0, 2, 3, 1))
    we_in = enc_weight[0, 0]
    wd_in = jnp.transpose(dec_weight[0, :, :, 0, :], (0, 2, 1))
    smem = pltpu.SMEM
    vmem = pl.BlockSpec(memory_space=pltpu.VMEM)
    hbm = pl.BlockSpec(memory_space=pl.ANY)
    small = (lengths, clamp_values, active_blocks, attn_scale, mlp_scale, enc_bias, clamp_mode, clamp_index)
    big = (x_in, err_in, pat_in, wv_in, wo_in, we_in, wd_in)
    half = seq // 2
    kv_heads = out_proj.shape[1]
    dma = pltpu.SemaphoreType.DMA
    out_t, out_f = pl.pallas_call(
        functools.partial(kernel, sizes),
        out_shape=(pltpu.VMEM((width, rows), F32), pltpu.VMEM((rows, block), BF16)),
        in_specs=[hbm] * 15,
        out_specs=(vmem, vmem),
        scratch_shapes=[(smem if i < 3 else pltpu.VMEM)(a.shape, a.dtype) for i, a in enumerate(small)]
        + [pltpu.VMEM(a.shape, a.dtype) for a in big]
        + [
            pltpu.VMEM((prompts, seq, width), F32),
            pltpu.VMEM((prompts, feat_n, seq, width), BF16),
            pltpu.VMEM((prompts, seq, width), BF16),
            pltpu.VMEM((rows, width), BF16),
            pltpu.VMEM((kv_heads, prompts, per_group * seq, seq), BF16),
            pltpu.VMEM((prompts, seq, kv), F32),
            pltpu.VMEM((prompts, seq, kv), F32),
            pltpu.VMEM((prompts, feat_n, seq, kv), BF16),
            pltpu.VMEM((prompts, 2, half, block), F32),
            pltpu.VMEM((prompts, 2 * feat_n, half, block), BF16),
            pltpu.VMEM((prompts, 2 * feat_n, half, block), BF16),
            pltpu.VMEM((prompts, 2 * feat_n, half, block), BF16),
            pltpu.VMEM((prompts, layers, seq, width), F32),
            pltpu.VMEM((prompts, layers, seq, width), F32),
            pltpu.VMEM((rows, width), F32),
            pltpu.VMEM((rows, width), F32),
        ]
        + [pltpu.VMEM((feat_n, width, block), BF16)] * 3
        + [
            dma((4,)), pltpu.SemaphoreType.REGULAR((2,)), dma((1,)), dma((prompts,)), dma((prompts, 2)), dma((prompts, feat_n)), dma((prompts,)),
            dma((prompts, feat_n)), dma((prompts,)), dma((prompts,)), dma((prompts, layers - 1)),
            dma((3, feat_n)), dma((shares, feat_n)),
        ],
        compiler_params=pltpu.CompilerParams(collective_id=0, has_side_effects=True),
    )(*small, *big)
    out_t, out_f = (pltpu.with_memory_space_constraint(a, pltpu.VMEM) for a in (out_t, out_f))
    out_t, out_f = pl.pallas_call(
        store,
        out_shape=(
            jax.ShapeDtypeStruct((width, rows), F32),
            jax.ShapeDtypeStruct((rows, block), BF16),
        ),
        in_specs=[vmem, vmem],
        out_specs=(hbm, hbm),
        scratch_shapes=[dma((2,))],
    )(out_t, out_f)
    return out_t.T[None, :, None, :], out_f[None]


def solution(mesh):
    return jax.shard_map(
        local,
        mesh=mesh,
        in_specs=(
            P("groups", "tok", "feat"),
            P("layer", "groups"),
            P("layer", "groups"),
            P("layer", None, "groups", None, None),
            P("groups"),
            P("layer", "tok", None, "feat"),
            P("layer", None, None, None, "tok", "feat"),
            P("layer", "tok", None, "feat"),
            P("layer", "feat"),
            P("layer", None, None, "tok", "feat"),
            P("layer", "groups", "tok", "feat"),
            P("layer", "feat"),
            P("layer", "feat"),
            P(),
            P("layer", "feat"),
        ),
        out_specs=(P("layer", "groups", "tok", "feat"), P("layer", "groups", "feat")),
        check_vma=False,
    )
```

```python
import functools

import jax
import jax.numpy as jnp
from jax import lax
from jax.experimental import pallas as pl
from jax.experimental.pallas import tpu as pltpu
from jax.sharding import PartitionSpec as P

F32 = jnp.float32
BF16 = jnp.bfloat16
NT = (((1,), (1,)), ((), ()))


def column(row):
    rows = row.shape[1]
    return jnp.transpose(jnp.broadcast_to(row, (128, rows)))[:, 0:1]


def kernel(
    sizes,
    lengths_in, table_in, chosen_in, attn_in, mlp_in, bias_in, mode_in, index_in,
    x_in, err_in, pat_in, wv_in, wo_in, we_in, wd_in,
    out_ref, feat_ref,
    lengths, table, chosen, scale_attn, scale_mlp, bias, mode_row, index_row,
    x_t, err_t, pat, wv, wo, we, wd,
    xbuf, slots, nbuf, normed, masked, part_v, part_v2, vals, part_e, e_out, e_in, feats,
    acc_in, acc_out, att, err, wek, relay_in, relay_mid,
    local_sem, ready, sent, up_sent, own_recv, xs_recv, t_recv, v_recv, vh_recv, m_recv, f_recv, a_recv, w_recv, b_recv,
):
    layers, feat_n, seq, prompts, head_dim, per_group, kv, width, block, rows, entries, shares = sizes
    half = seq // 2
    me_g = lax.axis_index("groups")
    me_l = lax.axis_index("layer")
    me_f = lax.axis_index("feat")
    me_t = lax.axis_index("tok")
    has_next = me_l < layers - 1
    has_prev = me_l > 0
    is_first = jnp.logical_not(has_prev)
    other = 1 - me_t
    nxt = jnp.minimum(me_l + 1, layers - 1)
    prv = jnp.maximum(me_l - 1, 0)
    streams = range(prompts)
    at_end = jnp.logical_or(me_f == 0, me_f == feat_n - 1)
    order = sorted(range(feat_n), key=lambda s: abs(2 * s - feat_n + 1))
    low_side = 2 * me_f < feat_n
    both = jnp.logical_and

    loads = [
        pltpu.make_async_copy(src, dst, local_sem.at[min(i, 2)])
        for i, (src, dst) in enumerate(
            (
                (x_in, x_t), (we_in, we), (attn_in, scale_attn), (lengths_in, lengths), (table_in, table),
                (chosen_in, chosen), (mlp_in, scale_mlp), (bias_in, bias), (mode_in, mode_row),
                (index_in, index_row), (wv_in, wv), (pat_in, pat), (wo_in, wo), (wd_in, wd), (err_in, err_t),
            )
        )
    ]
    for load in loads:
        load.start()
    l_x, l_we = loads[:2]

    barrier = pltpu.get_barrier_semaphore()
    mesh_id = pl.DeviceIdType.MESH

    def greet(where):
        pl.semaphore_signal(barrier, inc=1, device_id=where, device_id_type=mesh_id)

    for j in range(1, feat_n):
        for t in range(2):
            greet({"feat": (me_f + j) % feat_n, "tok": t})
    for s in range(feat_n):
        pl.when(both(has_next, jnp.abs(me_f - s) != 1))(lambda: greet({"layer": nxt, "feat": s}))
    for g in range(1, shares):
        pl.when(is_first)(lambda: greet({"groups": (me_g + g) % shares, "layer": nxt}))
    greet({"tok": other})

    def send(src, dst, rs, where):
        return pltpu.make_async_remote_copy(
            src_ref=src, dst_ref=dst, send_sem=sent.at[0], recv_sem=rs, device_id=where, device_id_type=mesh_id
        )

    def peer(j):
        return (me_f + j) % feat_n

    def far(k):
        down = feat_n - 1 - k
        return jnp.where(low_side, down - jnp.where(down <= me_f, 1, 0), k + jnp.where(k >= me_f, 1, 0))

    def part(p):
        return pl.ds(p * seq, seq)

    pending = []

    def launch(copy, cond=None):
        pending.append((copy, cond))
        if cond is None:
            copy.start()
        else:
            pl.when(cond)(copy.start)

    def landed(ref, rs):
        send(ref, ref, rs, {"tok": other}).wait_recv()

    l_x.wait()
    x_rows = jnp.transpose(x_t[...])

    @pl.when(is_first)
    def _():
        x_half = x_rows.astype(BF16)
        for p in streams:
            slots[p, me_f] = x_half[p * seq : (p + 1) * seq]
            xbuf[p] = x_rows[p * seq : (p + 1) * seq]

    met = feat_n - 2 + jnp.where(at_end, 1, 0)
    second = jnp.minimum(me_l, 1) * (1 - jnp.minimum(me_l // 2, 1))
    pl.semaphore_wait(barrier, 2 * feat_n - 1 + jnp.minimum(me_l, 1) * met + second * (shares - 1))
    for s in range(feat_n):
        @pl.when(both(has_prev, jnp.abs(me_f - s) != 1))
        def _():
            slot = jnp.minimum(jnp.abs(me_f - s), 1)
            pl.semaphore_signal(ready.at[slot], inc=1, device_id={"layer": prv, "feat": s}, device_id_type=mesh_id)

    def share_x(p, step, cond):
        to = me_f + step
        cond = both(both(to >= 0, to < feat_n), cond)
        to = jnp.clip(to, 0, feat_n - 1)
        slot = slots.at[p, me_f]
        launch(send(slot, slot, xs_recv.at[p, me_f], {"feat": to}), cond)

    def x_landed(p, s):
        landed(slots.at[p, s], xs_recv.at[p, s])

    def share_first(p):
        for step in (2, -2, 1, -1):
            share_x(p, step, is_first)

    share_first(0)

    def we_rows(s):
        return we.at[pl.ds(pl.multiple_of(s * width, 16), width)]

    l_we.wait()
    own_rows = pltpu.make_async_copy(we_rows(me_f), wek.at[me_f], local_sem.at[3])
    own_rows.start()
    share = width // shares
    my_share = me_g if shares > 1 else 0
    front = pl.ds(0, share)
    first_up = [
        send(
            we.at[pl.ds(pl.multiple_of(peer(j) * width + my_share * share, 16), share)],
            relay_in.at[peer(j), front], w_recv.at[0, peer(j)], {"layer": nxt},
        )
        for j in range(1, feat_n)
    ]
    across = [
        send(
            relay_in.at[peer(j), front], relay_mid.at[me_f, front],
            w_recv.at[1, me_f], {"feat": peer(j)},
        )
        for j in range(1, feat_n)
    ]
    back = [
        [
            send(
                relay_mid.at[peer(j), front],
                wek.at[peer(j), pl.ds(pl.multiple_of(my_share * share, 16), share)],
                b_recv.at[my_share, peer(j)],
                {"layer": prv, "groups": (me_g + g) % shares} if g else {"layer": prv},
            )
            for g in range(shares)
        ]
        for j in range(1, feat_n)
    ]
    direct = [
        send(we_rows(peer(j)), wek.at[me_f], w_recv.at[2, me_f], {"feat": peer(j)})
        for j in range(1, feat_n)
    ]

    def w_arrived(ref, stage, s):
        part_ref = ref.at[s, front] if stage < 2 else ref.at[s]
        landed(part_ref, w_recv.at[stage, s])

    def distant(j):
        return jnp.abs(peer(j) - me_f) > 1

    def next_to(j):
        return jnp.abs(peer(j) - me_f) == 1

    pl.when(has_next)(lambda: pl.semaphore_wait(ready.at[0], 1))
    for j in range(1, feat_n):
        launch(first_up[j - 1], both(is_first, distant(j)))
    for j in range(1, feat_n):
        relays = both(me_l == 1, distant(j))
        pl.when(relays)(lambda: w_arrived(relay_in, 0, peer(j)))
        launch(across[j - 1], relays)
    for j in range(1, feat_n):
        relays = both(me_l == 1, distant(j))
        pl.when(relays)(lambda: w_arrived(relay_mid, 1, peer(j)))
        for copy in back[j - 1]:
            launch(copy, relays)
    for j in range(1, feat_n):
        launch(direct[j - 1], has_prev)

    for load in loads[2:]:
        load.wait()
    ids = lax.broadcasted_iota(jnp.int32, (half, 1), 0) + me_t * half
    lives = [ids < lengths[p] for p in streams]
    which = jnp.zeros((1, block), jnp.int32) + chosen[0, 0]
    modes = picks = jnp.zeros((1, block), jnp.int32)
    for b in range(mode_row.shape[1] // block):
        here = which == b
        modes = jnp.where(here, mode_row[:, b * block : (b + 1) * block], modes)
        picks = jnp.where(here, index_row[:, b * block : (b + 1) * block], picks)
    levels = jnp.zeros((1, block), F32)
    for v in range(entries):
        levels = jnp.where(picks == v, table[v], levels)
    attn_col = column(scale_attn[...])
    mlp_col = column(scale_mlp[...])
    shift = bias[...]
    err[...] = jnp.transpose(err_t[...])
    q_ids = lax.broadcasted_iota(jnp.int32, (seq, seq), 0)
    k_ids = lax.broadcasted_iota(jnp.int32, (seq, seq), 1)
    for p in streams:
        keep = both(k_ids <= q_ids, k_ids < lengths[p])
        for h in range(pat.shape[0]):
            masked[h // per_group, p, pl.ds(h % per_group * seq, seq), :] = jnp.where(
                keep, pat[h, p].astype(F32), 0.0
            ).astype(BF16)
        e_in[p, 2 * me_f + me_t] = jnp.zeros((half, block), BF16)
    own_rows.wait()

    for p in streams:
        for h in range(2):
            slot = slots.at[p, me_f, pl.ds(h * half, half)]
            pl.when(has_prev)(lambda: landed(slot, own_recv.at[p, h]))
            for step in (1, -1):
                to = me_f + step
                inside = both(has_prev, both(to >= 0, to < feat_n))
                launch(send(slot, slot, xs_recv.at[p, me_f], {"feat": jnp.clip(to, 0, feat_n - 1)}), inside)

        @pl.when(has_prev)
        def _():
            xbuf[p] = slots[p, me_f].astype(F32)

    def arrival(k):
        return jnp.where(at_end, far(feat_n - 1 - k), far(k - 1)) if k else me_f

    def splits(p):
        return p + 1 < prompts

    def rows_of(p, s, t):
        return vals.at[p, s, pl.ds(pl.multiple_of(t * half, 16), half)]

    def v_sends(p):
        if splits(p):
            mine, arrive = rows_of(p, me_f, me_t), vh_recv.at[p, me_f, me_t]
        else:
            mine, arrive = vals.at[p, me_f], v_recv.at[p, me_f]
        return [send(mine, mine, arrive, {"feat": far(k)}) for k in range(feat_n - 1)]

    def v_finish(p, cond):
        @pl.when(cond)
        def _():
            landed(part_v2.at[p], t_recv.at[p])
            vals[p, me_f] = (part_v[p] + part_v2[p]).astype(BF16)
            for copy in v_sends(p):
                copy.start()

    relaying = both(is_first, jnp.logical_not(at_end))
    for p in streams:
        pending.extend((copy, None) for copy in v_sends(p))
        total = jnp.zeros((seq, kv), F32)
        if p:
            v_finish(p - 1, jnp.logical_not(relaying))
        for k in range(feat_n):
            s = arrival(k)
            if k:
                x_landed(p, s)
                for step in (1, -1):
                    to = me_f + step
                    inside = both(to >= 0, to < feat_n)
                    relays = both(is_first, both(inside, (to - s) * step > 2))
                    to = jnp.clip(to, 0, feat_n - 1)
                    launch(send(slots.at[p, s], slots.at[p, s], xs_recv.at[p, s], {"feat": to}), relays)
            if k == 1:
                if p + 1 < prompts:
                    share_first(p + 1)
                if p:
                    v_finish(p - 1, relaying)
                if p + 1 == prompts:
                    for j in range(1, feat_n):
                        launch(direct[j - 1], both(is_first, next_to(j)))
            from_rows = pl.ds(pl.multiple_of(s * width, 16), width)
            total += jnp.dot(slots[p, s], wv[from_rows, :], preferred_element_type=F32)
        total *= attn_col[p * seq : (p + 1) * seq]
        part_v[p] = total
        launch(send(part_v.at[p], part_v2.at[p], t_recv.at[p], {"tok": other}))
    v_finish(prompts - 1, me_f >= 0)

    def encode(p):
        for k in range(feat_n):
            to = far(k) if k < feat_n - 1 else me_f
            result = jnp.dot(normed[part(p), :], wek[to], preferred_element_type=F32).reshape(2, half, block)
            for t in range(2):
                e_out[p, 2 * k + t] = result[t].astype(BF16)
                if k < feat_n - 1:
                    launch(e_send(p, k, t))
            if k == feat_n - 1:
                part_e[p] = result
                launch(e_swap(p))

    def e_send(p, k, t):
        return send(e_out.at[p, 2 * k + t], e_in.at[p, 2 * me_f + me_t], m_recv.at[p], {"feat": far(k), "tok": t})

    def e_swap(p):
        mine = 2 * (feat_n - 1) + other
        return send(e_out.at[p, mine], e_in.at[p, 2 * me_f + me_t], m_recv.at[p], {"tok": other})

    def hand_over(p, s):
        got, arrive = rows_of(p, s, me_t), vh_recv.at[p, s, me_t]
        pl.when(me_f != s)(lambda: landed(got, arrive))
        launch(send(got, got, arrive, {"tok": other}), me_f != s)

    for p in streams:
        total = jnp.zeros((seq, width), F32)
        if splits(p):
            hand_over(p, order[0])
        for n, s in enumerate(order):
            if splits(p):
                if n + 1 < feat_n:
                    hand_over(p, order[n + 1])
                pl.when(me_f != s)(lambda: landed(rows_of(p, s, other), vh_recv.at[p, s, other]))
            else:
                pl.when(me_f != s)(lambda: landed(vals.at[p, s], v_recv.at[p, s]))
            group = s * kv // head_dim
            d0 = s * kv % head_dim
            heads = jnp.dot(masked[group, p], vals[p, s], preferred_element_type=F32).astype(BF16)
            for u in range(per_group):
                total += lax.dot_general(
                    heads[u * seq : (u + 1) * seq], wo[group, u, :, pl.ds(d0, kv)], NT, preferred_element_type=F32
                )
        middle = xbuf[p] + total
        normed[part(p), :] = (middle * mlp_col[p * seq : (p + 1) * seq]).astype(BF16)
        att[part(p), :] = middle + err[part(p), :]
        if p == 0:
            for s in range(feat_n):
                apart = jnp.abs(me_f - s)
                straight = jnp.logical_or(both(has_prev, apart > 0), apart == 1)
                pl.when(straight)(lambda: w_arrived(wek, 2, s))
                for g in range(shares):
                    pl.when(both(is_first, apart > 1))(
                        lambda: landed(wek.at[s, pl.ds(g * share, share)], b_recv.at[g, s])
                    )
        encode(p)

    def await_others(ref, rs):
        landed(ref.at[pl.ds(0, 2 * feat_n - 1)], rs)

    for p in streams:
        await_others(e_in.at[p], m_recv.at[p])
        preact = part_e[p, me_t] + shift
        for s in range(2 * feat_n):
            preact += e_in[p, s].astype(F32)
        active = jnp.maximum(preact, 0.0)
        clamped = jnp.where(modes == 1, levels, jnp.where(modes == 2, active * levels, active))
        here = 2 * me_f + me_t
        feats[p, here] = jnp.where(lives[p], clamped, 0.0).astype(BF16)
        mine = feats.at[p, here]
        for k in range(feat_n - 1):
            for t in range(2):
                launch(send(mine, mine, f_recv.at[p], {"feat": far(k), "tok": t}))
        launch(send(mine, mine, f_recv.at[p], {"tok": other}))

    pair = 2 if feat_n % 2 == 0 else 1

    def decode(p, t, total):
        for s in range(0, feat_n, pair):
            lhs = [feats[p, 2 * i : 2 * i + 2].reshape(seq, block) for i in range(s, s + pair)]
            total += lax.dot_general(
                jnp.concatenate(lhs, axis=1), wd[t, :, pl.ds(s * block, pair * block)], NT,
                preferred_element_type=F32,
            )
        return total

    def x_up(p, h):
        part_h = pl.ds(h * half, half)
        return pltpu.make_async_remote_copy(
            src_ref=nbuf.at[p, part_h], dst_ref=slots.at[p, me_f, part_h], send_sem=up_sent.at[p],
            recv_sem=own_recv.at[p, h], device_id={"layer": nxt}, device_id_type=mesh_id,
        )

    def acc_copy(p, t):
        return send(acc_out.at[p, t], acc_in.at[p, t], a_recv.at[p, t - 1], {"layer": nxt})

    pl.when(has_next)(lambda: pl.semaphore_wait(ready.at[1], met - 1))
    for p in streams:
        @pl.when(has_prev)
        def _():
            for t in range(1, layers):
                @pl.when(t >= me_l)
                def _():
                    acc_copy(p, t).wait_recv()
            att[part(p), :] += acc_in[p, me_l]

        total = att[part(p), :]
        await_others(feats.at[p], f_recv.at[p])
        att[part(p), :] = decode(p, me_l, total)
        feat_ref[part(p), :] = feats[p, pl.ds(2 * me_f, 2)].reshape(seq, block)

        @pl.when(has_next)
        def _():
            nbuf[p] = att[part(p), :].astype(BF16)

        for h in range(2):
            pl.when(has_next)(x_up(p, h).start)
        for k in range(feat_n - 1):
            to = far(k)
            launch(
                send(nbuf.at[p], slots.at[p, me_f], xs_recv.at[p, me_f], {"layer": nxt, "feat": to}),
                both(has_next, jnp.abs(to - me_f) > 1),
            )

    @pl.when(has_next)
    def _():
        for p in streams:
            for t in range(1, layers):
                @pl.when(t > me_l)
                def _():
                    rest = att[part(p), :] - nbuf[p].astype(F32)
                    total = jnp.where(me_l + 1 == t, rest, 0.0)
                    acc_out[p, t] = decode(p, t, total)

                    @pl.when(has_prev)
                    def _():
                        acc_out[p, t] += acc_in[p, t]

        for p in streams:
            for h in range(2):
                x_up(p, h).wait_send()
        for p in streams:
            for t in range(1, layers):
                pl.when(t > me_l)(lambda: acc_copy(p, t).start())

    out_ref[...] = jnp.transpose(att[...])

    for copy, cond in pending:
        if cond is None:
            copy.wait_send()
        else:
            pl.when(cond)(copy.wait_send)

    @pl.when(has_next)
    def _():
        for p in streams:
            for t in range(1, layers):
                @pl.when(t > me_l)
                def _():
                    acc_copy(p, t).wait_send()


def store(x_ref, f_ref, out_ref, feat_ref, sems):
    copies = [
        pltpu.make_async_copy(x_ref, out_ref, sems.at[0]),
        pltpu.make_async_copy(f_ref, feat_ref, sems.at[1]),
    ]
    for copy in copies:
        copy.start()
    for copy in copies:
        copy.wait()


def local(
    residual_in, attn_scale, mlp_scale, patterns, lengths, value_proj, out_proj, enc_weight, enc_bias,
    dec_weight, errors, clamp_mode, clamp_index, clamp_values, active_blocks,
):
    layers = lax.axis_size("layer")
    feat_n = lax.axis_size("feat")
    prompts, seq = patterns.shape[2], patterns.shape[3]
    head_dim, per_group = out_proj.shape[2], out_proj.shape[3]
    kv = value_proj.shape[3]
    rows, _, width = residual_in.shape
    block = enc_bias.shape[1]
    entries = clamp_values.shape[0]
    groups = lax.axis_size("groups")
    shares = groups if width % (16 * groups) == 0 else 1
    sizes = (layers, feat_n, seq, prompts, head_dim, per_group, kv, width, block, rows, entries, shares)
    x_in = residual_in[:, 0, :].T
    err_in = errors[0, :, 0, :].T
    pat_in = patterns[0]
    wv_in = value_proj[0, 0]
    wo_in = jnp.transpose(out_proj[0, :, :, :, 0, :], (0, 2, 3, 1))
    we_in = enc_weight[0, 0]
    wd_in = jnp.transpose(dec_weight[0, :, :, 0, :], (0, 2, 1))
    smem = pltpu.SMEM
    vmem = pl.BlockSpec(memory_space=pltpu.VMEM)
    hbm = pl.BlockSpec(memory_space=pl.ANY)
    small = (lengths, clamp_values, active_blocks, attn_scale, mlp_scale, enc_bias, clamp_mode, clamp_index)
    big = (x_in, err_in, pat_in, wv_in, wo_in, we_in, wd_in)
    half = seq // 2
    kv_heads = out_proj.shape[1]
    dma = pltpu.SemaphoreType.DMA
    out_t, out_f = pl.pallas_call(
        functools.partial(kernel, sizes),
        out_shape=(pltpu.VMEM((width, rows), F32), pltpu.VMEM((rows, block), BF16)),
        in_specs=[hbm] * 15,
        out_specs=(vmem, vmem),
        scratch_shapes=[(smem if i < 3 else pltpu.VMEM)(a.shape, a.dtype) for i, a in enumerate(small)]
        + [pltpu.VMEM(a.shape, a.dtype) for a in big]
        + [
            pltpu.VMEM((prompts, seq, width), F32),
            pltpu.VMEM((prompts, feat_n, seq, width), BF16),
            pltpu.VMEM((prompts, seq, width), BF16),
            pltpu.VMEM((rows, width), BF16),
            pltpu.VMEM((kv_heads, prompts, per_group * seq, seq), BF16),
            pltpu.VMEM((prompts, seq, kv), F32),
            pltpu.VMEM((prompts, seq, kv), F32),
            pltpu.VMEM((prompts, feat_n, seq, kv), BF16),
            pltpu.VMEM((prompts, 2, half, block), F32),
            pltpu.VMEM((prompts, 2 * feat_n, half, block), BF16),
            pltpu.VMEM((prompts, 2 * feat_n, half, block), BF16),
            pltpu.VMEM((prompts, 2 * feat_n, half, block), BF16),
            pltpu.VMEM((prompts, layers, seq, width), F32),
            pltpu.VMEM((prompts, layers, seq, width), F32),
            pltpu.VMEM((rows, width), F32),
            pltpu.VMEM((rows, width), F32),
        ]
        + [pltpu.VMEM((feat_n, width, block), BF16)] * 3
        + [
            dma((4,)), pltpu.SemaphoreType.REGULAR((2,)), dma((1,)), dma((prompts,)), dma((prompts, 2)), dma((prompts, feat_n)), dma((prompts,)),
            dma((prompts, feat_n)), dma((prompts, feat_n, 2)), dma((prompts,)), dma((prompts,)), dma((prompts, layers - 1)),
            dma((3, feat_n)), dma((shares, feat_n)),
        ],
        compiler_params=pltpu.CompilerParams(collective_id=0, has_side_effects=True),
    )(*small, *big)
    out_t, out_f = (pltpu.with_memory_space_constraint(a, pltpu.VMEM) for a in (out_t, out_f))
    out_t, out_f = pl.pallas_call(
        store,
        out_shape=(
            jax.ShapeDtypeStruct((width, rows), F32),
            jax.ShapeDtypeStruct((rows, block), BF16),
        ),
        in_specs=[vmem, vmem],
        out_specs=(hbm, hbm),
        scratch_shapes=[dma((2,))],
    )(out_t, out_f)
    return out_t.T[None, :, None, :], out_f[None]


def solution(mesh):
    return jax.shard_map(
        local,
        mesh=mesh,
        in_specs=(
            P("groups", "tok", "feat"),
            P("layer", "groups"),
            P("layer", "groups"),
            P("layer", None, "groups", None, None),
            P("groups"),
            P("layer", "tok", None, "feat"),
            P("layer", None, None, None, "tok", "feat"),
            P("layer", "tok", None, "feat"),
            P("layer", "feat"),
            P("layer", None, None, "tok", "feat"),
            P("layer", "groups", "tok", "feat"),
            P("layer", "feat"),
            P("layer", "feat"),
            P(),
            P("layer", "feat"),
        ),
        out_specs=(P("layer", "groups", "tok", "feat"), P("layer", "groups", "feat")),
        check_vma=False,
    )
```

```python
import functools

import jax
import jax.numpy as jnp
from jax import lax
from jax.experimental import pallas as pl
from jax.experimental.pallas import tpu as pltpu
from jax.sharding import PartitionSpec as P

F32 = jnp.float32
BF16 = jnp.bfloat16
NT = (((1,), (1,)), ((), ()))


def column(row):
    rows = row.shape[1]
    return jnp.transpose(jnp.broadcast_to(row, (128, rows)))[:, 0:1]


def kernel(
    sizes,
    lengths_in, table_in, chosen_in, attn_in, mlp_in, bias_in, mode_in, index_in,
    x_in, err_in, pat_in, wv_in, wo_in, we_in, wd_in,
    out_ref, feat_ref,
    lengths, table, chosen, scale_attn, scale_mlp, bias, mode_row, index_row,
    x_t, err_t, pat, wv, wo, we, wd,
    xbuf, slots, nbuf, normed, masked, part_v, part_v2, vals, part_e, e_out, e_in, feats,
    acc_in, acc_out, att, err, wek, relay_in, relay_mid,
    local_sem, ready, sent, up_sent, own_recv, xs_recv, t_recv, v_recv, vh_recv, m_recv, f_recv, a_recv, w_recv, b_recv,
):
    layers, feat_n, seq, prompts, head_dim, per_group, kv, width, block, rows, entries, shares = sizes
    half = seq // 2
    me_g = lax.axis_index("groups")
    me_l = lax.axis_index("layer")
    me_f = lax.axis_index("feat")
    me_t = lax.axis_index("tok")
    has_next = me_l < layers - 1
    has_prev = me_l > 0
    is_first = jnp.logical_not(has_prev)
    other = 1 - me_t
    nxt = jnp.minimum(me_l + 1, layers - 1)
    prv = jnp.maximum(me_l - 1, 0)
    streams = range(prompts)
    at_end = jnp.logical_or(me_f == 0, me_f == feat_n - 1)
    order = sorted(range(feat_n), key=lambda s: abs(2 * s - feat_n + 1))
    low_side = 2 * me_f < feat_n
    both = jnp.logical_and

    loads = [
        pltpu.make_async_copy(src, dst, local_sem.at[min(i, 2)])
        for i, (src, dst) in enumerate(
            (
                (x_in, x_t), (we_in, we), (attn_in, scale_attn), (lengths_in, lengths), (table_in, table),
                (chosen_in, chosen), (mlp_in, scale_mlp), (bias_in, bias), (mode_in, mode_row),
                (index_in, index_row), (wv_in, wv), (pat_in, pat), (wo_in, wo), (wd_in, wd), (err_in, err_t),
            )
        )
    ]
    for load in loads:
        load.start()
    l_x, l_we = loads[:2]

    barrier = pltpu.get_barrier_semaphore()
    mesh_id = pl.DeviceIdType.MESH

    def greet(where):
        pl.semaphore_signal(barrier, inc=1, device_id=where, device_id_type=mesh_id)

    for j in range(1, feat_n):
        for t in range(2):
            greet({"feat": (me_f + j) % feat_n, "tok": t})
    for s in range(feat_n):
        pl.when(both(has_next, jnp.abs(me_f - s) != 1))(lambda: greet({"layer": nxt, "feat": s}))
    for g in range(1, shares):
        pl.when(is_first)(lambda: greet({"groups": (me_g + g) % shares, "layer": nxt}))
    greet({"tok": other})

    def send(src, dst, rs, where):
        return pltpu.make_async_remote_copy(
            src_ref=src, dst_ref=dst, send_sem=sent.at[0], recv_sem=rs, device_id=where, device_id_type=mesh_id
        )

    def peer(j):
        return (me_f + j) % feat_n

    def far(k):
        down = feat_n - 1 - k
        return jnp.where(low_side, down - jnp.where(down <= me_f, 1, 0), k + jnp.where(k >= me_f, 1, 0))

    def part(p):
        return pl.ds(p * seq, seq)

    pending = []

    def launch(copy, cond=None):
        pending.append((copy, cond))
        if cond is None:
            copy.start()
        else:
            pl.when(cond)(copy.start)

    def landed(ref, rs):
        send(ref, ref, rs, {"tok": other}).wait_recv()

    l_x.wait()
    x_rows = jnp.transpose(x_t[...])

    @pl.when(is_first)
    def _():
        x_half = x_rows.astype(BF16)
        for p in streams:
            slots[p, me_f] = x_half[p * seq : (p + 1) * seq]
            xbuf[p] = x_rows[p * seq : (p + 1) * seq]

    met = feat_n - 2 + jnp.where(at_end, 1, 0)
    second = jnp.minimum(me_l, 1) * (1 - jnp.minimum(me_l // 2, 1))
    pl.semaphore_wait(barrier, 2 * feat_n - 1 + jnp.minimum(me_l, 1) * met + second * (shares - 1))
    for s in range(feat_n):
        @pl.when(both(has_prev, jnp.abs(me_f - s) != 1))
        def _():
            slot = jnp.minimum(jnp.abs(me_f - s), 1)
            pl.semaphore_signal(ready.at[slot], inc=1, device_id={"layer": prv, "feat": s}, device_id_type=mesh_id)

    def share_x(p, step, cond):
        to = me_f + step
        cond = both(both(to >= 0, to < feat_n), cond)
        to = jnp.clip(to, 0, feat_n - 1)
        slot = slots.at[p, me_f]
        launch(send(slot, slot, xs_recv.at[p, me_f], {"feat": to}), cond)

    def x_landed(p, s):
        landed(slots.at[p, s], xs_recv.at[p, s])

    def share_first(p):
        for step in (2, -2, 1, -1):
            share_x(p, step, is_first)

    share_first(0)

    def we_rows(s):
        return we.at[pl.ds(pl.multiple_of(s * width, 16), width)]

    l_we.wait()
    own_rows = pltpu.make_async_copy(we_rows(me_f), wek.at[me_f], local_sem.at[3])
    own_rows.start()
    share = width // shares
    my_share = me_g if shares > 1 else 0
    front = pl.ds(0, share)
    first_up = [
        send(
            we.at[pl.ds(pl.multiple_of(peer(j) * width + my_share * share, 16), share)],
            relay_in.at[peer(j), front], w_recv.at[0, peer(j)], {"layer": nxt},
        )
        for j in range(1, feat_n)
    ]
    across = [
        send(
            relay_in.at[peer(j), front], relay_mid.at[me_f, front],
            w_recv.at[1, me_f], {"feat": peer(j)},
        )
        for j in range(1, feat_n)
    ]
    back = [
        [
            send(
                relay_mid.at[peer(j), front],
                wek.at[peer(j), pl.ds(pl.multiple_of(my_share * share, 16), share)],
                b_recv.at[my_share, peer(j)],
                {"layer": prv, "groups": (me_g + g) % shares} if g else {"layer": prv},
            )
            for g in range(shares)
        ]
        for j in range(1, feat_n)
    ]
    direct = [
        send(we_rows(peer(j)), wek.at[me_f], w_recv.at[2, me_f], {"feat": peer(j)})
        for j in range(1, feat_n)
    ]

    def w_arrived(ref, stage, s):
        part_ref = ref.at[s, front] if stage < 2 else ref.at[s]
        landed(part_ref, w_recv.at[stage, s])

    def distant(j):
        return jnp.abs(peer(j) - me_f) > 1

    def next_to(j):
        return jnp.abs(peer(j) - me_f) == 1

    pl.when(has_next)(lambda: pl.semaphore_wait(ready.at[0], 1))
    for j in range(1, feat_n):
        launch(first_up[j - 1], both(is_first, distant(j)))
    for j in range(1, feat_n):
        relays = both(me_l == 1, distant(j))
        pl.when(relays)(lambda: w_arrived(relay_in, 0, peer(j)))
        launch(across[j - 1], relays)
    for j in range(1, feat_n):
        relays = both(me_l == 1, distant(j))
        pl.when(relays)(lambda: w_arrived(relay_mid, 1, peer(j)))
        for copy in back[j - 1]:
            launch(copy, relays)
    for j in range(1, feat_n):
        launch(direct[j - 1], has_prev)

    for load in loads[2:]:
        load.wait()
    ids = lax.broadcasted_iota(jnp.int32, (half, 1), 0) + me_t * half
    lives = [ids < lengths[p] for p in streams]
    which = jnp.zeros((1, block), jnp.int32) + chosen[0, 0]
    modes = picks = jnp.zeros((1, block), jnp.int32)
    for b in range(mode_row.shape[1] // block):
        here = which == b
        modes = jnp.where(here, mode_row[:, b * block : (b + 1) * block], modes)
        picks = jnp.where(here, index_row[:, b * block : (b + 1) * block], picks)
    levels = jnp.zeros((1, block), F32)
    for v in range(entries):
        levels = jnp.where(picks == v, table[v], levels)
    attn_col = column(scale_attn[...])
    mlp_col = column(scale_mlp[...])
    shift = bias[...]
    err[...] = jnp.transpose(err_t[...])
    q_ids = lax.broadcasted_iota(jnp.int32, (seq, seq), 0)
    k_ids = lax.broadcasted_iota(jnp.int32, (seq, seq), 1)
    for p in streams:
        keep = both(k_ids <= q_ids, k_ids < lengths[p])
        for h in range(pat.shape[0]):
            masked[h // per_group, p, pl.ds(h % per_group * seq, seq), :] = jnp.where(
                keep, pat[h, p].astype(F32), 0.0
            ).astype(BF16)
        e_in[p, 2 * me_f + me_t] = jnp.zeros((half, block), BF16)
    own_rows.wait()

    for p in streams:
        for h in range(2):
            slot = slots.at[p, me_f, pl.ds(h * half, half)]
            pl.when(has_prev)(lambda: landed(slot, own_recv.at[p, h]))
            for step in (1, -1):
                to = me_f + step
                inside = both(has_prev, both(to >= 0, to < feat_n))
                launch(send(slot, slot, xs_recv.at[p, me_f], {"feat": jnp.clip(to, 0, feat_n - 1)}), inside)
            if p == 0:
                for k in range(feat_n - 1):
                    onward = both(jnp.abs(far(k) - me_f) > 1, jnp.logical_not(at_end))
                    launch(send(slot, slot, xs_recv.at[p, me_f], {"feat": far(k)}), both(has_prev, onward))

        @pl.when(has_prev)
        def _():
            xbuf[p] = slots[p, me_f].astype(F32)

    def arrival(k):
        return jnp.where(at_end, far(feat_n - 1 - k), far(k - 1)) if k else me_f

    def splits(p):
        return p + 1 < prompts

    def rows_of(p, s, t):
        return vals.at[p, s, pl.ds(pl.multiple_of(t * half, 16), half)]

    def v_sends(p):
        if splits(p):
            mine, arrive = rows_of(p, me_f, me_t), vh_recv.at[p, me_f, me_t]
        else:
            mine, arrive = vals.at[p, me_f], v_recv.at[p, me_f]
        return [send(mine, mine, arrive, {"feat": far(k)}) for k in range(feat_n - 1)]

    def v_finish(p, cond):
        @pl.when(cond)
        def _():
            landed(part_v2.at[p], t_recv.at[p])
            vals[p, me_f] = (part_v[p] + part_v2[p]).astype(BF16)
            for copy in v_sends(p):
                copy.start()

    relaying = both(is_first, jnp.logical_not(at_end))
    for p in streams:
        pending.extend((copy, None) for copy in v_sends(p))
        total = jnp.zeros((seq, kv), F32)
        if p:
            v_finish(p - 1, jnp.logical_not(relaying))
        for k in range(feat_n):
            s = arrival(k)
            if k:
                x_landed(p, s)
                for step in (1, -1):
                    to = me_f + step
                    inside = both(to >= 0, to < feat_n)
                    relays = both(is_first, both(inside, (to - s) * step > 2))
                    to = jnp.clip(to, 0, feat_n - 1)
                    launch(send(slots.at[p, s], slots.at[p, s], xs_recv.at[p, s], {"feat": to}), relays)
            if k == 1:
                if p + 1 < prompts:
                    share_first(p + 1)
                if p:
                    v_finish(p - 1, relaying)
                if p + 1 == prompts:
                    for j in range(1, feat_n):
                        launch(direct[j - 1], both(is_first, next_to(j)))
            from_rows = pl.ds(pl.multiple_of(s * width, 16), width)
            total += jnp.dot(slots[p, s], wv[from_rows, :], preferred_element_type=F32)
        total *= attn_col[p * seq : (p + 1) * seq]
        part_v[p] = total
        launch(send(part_v.at[p], part_v2.at[p], t_recv.at[p], {"tok": other}))
    v_finish(prompts - 1, me_f >= 0)

    def encode(p):
        for k in range(feat_n):
            to = far(k) if k < feat_n - 1 else me_f
            result = jnp.dot(normed[part(p), :], wek[to], preferred_element_type=F32).reshape(2, half, block)
            for t in range(2):
                e_out[p, 2 * k + t] = result[t].astype(BF16)
                if k < feat_n - 1:
                    launch(e_send(p, k, t))
            if k == feat_n - 1:
                part_e[p] = result
                launch(e_swap(p))

    def e_send(p, k, t):
        return send(e_out.at[p, 2 * k + t], e_in.at[p, 2 * me_f + me_t], m_recv.at[p], {"feat": far(k), "tok": t})

    def e_swap(p):
        mine = 2 * (feat_n - 1) + other
        return send(e_out.at[p, mine], e_in.at[p, 2 * me_f + me_t], m_recv.at[p], {"tok": other})

    def hand_over(p, s):
        got, arrive = rows_of(p, s, me_t), vh_recv.at[p, s, me_t]
        pl.when(me_f != s)(lambda: landed(got, arrive))
        launch(send(got, got, arrive, {"tok": other}), me_f != s)

    for p in streams:
        total = jnp.zeros((seq, width), F32)
        if splits(p):
            hand_over(p, order[0])
        for n, s in enumerate(order):
            if splits(p):
                if n + 1 < feat_n:
                    hand_over(p, order[n + 1])
                pl.when(me_f != s)(lambda: landed(rows_of(p, s, other), vh_recv.at[p, s, other]))
            else:
                pl.when(me_f != s)(lambda: landed(vals.at[p, s], v_recv.at[p, s]))
            group = s * kv // head_dim
            d0 = s * kv % head_dim
            heads = jnp.dot(masked[group, p], vals[p, s], preferred_element_type=F32).astype(BF16)
            for u in range(per_group):
                total += lax.dot_general(
                    heads[u * seq : (u + 1) * seq], wo[group, u, :, pl.ds(d0, kv)], NT, preferred_element_type=F32
                )
        middle = xbuf[p] + total
        normed[part(p), :] = (middle * mlp_col[p * seq : (p + 1) * seq]).astype(BF16)
        att[part(p), :] = middle + err[part(p), :]
        if p == 0:
            for s in range(feat_n):
                apart = jnp.abs(me_f - s)
                straight = jnp.logical_or(both(has_prev, apart > 0), apart == 1)
                pl.when(straight)(lambda: w_arrived(wek, 2, s))
                for g in range(shares):
                    pl.when(both(is_first, apart > 1))(
                        lambda: landed(wek.at[s, pl.ds(g * share, share)], b_recv.at[g, s])
                    )
        encode(p)

    def await_others(ref, rs):
        landed(ref.at[pl.ds(0, 2 * feat_n - 1)], rs)

    for p in streams:
        await_others(e_in.at[p], m_recv.at[p])
        preact = part_e[p, me_t] + shift
        for s in range(2 * feat_n):
            preact += e_in[p, s].astype(F32)
        active = jnp.maximum(preact, 0.0)
        clamped = jnp.where(modes == 1, levels, jnp.where(modes == 2, active * levels, active))
        here = 2 * me_f + me_t
        feats[p, here] = jnp.where(lives[p], clamped, 0.0).astype(BF16)
        mine = feats.at[p, here]
        for k in range(feat_n - 1):
            for t in range(2):
                launch(send(mine, mine, f_recv.at[p], {"feat": far(k), "tok": t}))
        launch(send(mine, mine, f_recv.at[p], {"tok": other}))

    pair = 2 if feat_n % 2 == 0 else 1

    def decode(p, t, total):
        for s in range(0, feat_n, pair):
            lhs = [feats[p, 2 * i : 2 * i + 2].reshape(seq, block) for i in range(s, s + pair)]
            total += lax.dot_general(
                jnp.concatenate(lhs, axis=1), wd[t, :, pl.ds(s * block, pair * block)], NT,
                preferred_element_type=F32,
            )
        return total

    def x_up(p, h):
        part_h = pl.ds(h * half, half)
        return pltpu.make_async_remote_copy(
            src_ref=nbuf.at[p, part_h], dst_ref=slots.at[p, me_f, part_h], send_sem=up_sent.at[p],
            recv_sem=own_recv.at[p, h], device_id={"layer": nxt}, device_id_type=mesh_id,
        )

    def acc_copy(p, t):
        return send(acc_out.at[p, t], acc_in.at[p, t], a_recv.at[p, t - 1], {"layer": nxt})

    pl.when(has_next)(lambda: pl.semaphore_wait(ready.at[1], met - 1))
    for p in streams:
        @pl.when(has_prev)
        def _():
            for t in range(1, layers):
                @pl.when(t >= me_l)
                def _():
                    acc_copy(p, t).wait_recv()
            att[part(p), :] += acc_in[p, me_l]

        total = att[part(p), :]
        await_others(feats.at[p], f_recv.at[p])
        att[part(p), :] = decode(p, me_l, total)
        feat_ref[part(p), :] = feats[p, pl.ds(2 * me_f, 2)].reshape(seq, block)

        @pl.when(has_next)
        def _():
            nbuf[p] = att[part(p), :].astype(BF16)

        for h in range(2):
            pl.when(has_next)(x_up(p, h).start)
        for k in range(feat_n - 1):
            to = far(k)
            launch(
                send(nbuf.at[p], slots.at[p, me_f], xs_recv.at[p, me_f], {"layer": nxt, "feat": to}),
                both(both(has_next, jnp.abs(to - me_f) > 1), at_end if p == 0 else has_next),
            )

    @pl.when(has_next)
    def _():
        for p in streams:
            for t in range(1, layers):
                @pl.when(t > me_l)
                def _():
                    rest = att[part(p), :] - nbuf[p].astype(F32)
                    total = jnp.where(me_l + 1 == t, rest, 0.0)
                    acc_out[p, t] = decode(p, t, total)

                    @pl.when(has_prev)
                    def _():
                        acc_out[p, t] += acc_in[p, t]

        for p in streams:
            for h in range(2):
                x_up(p, h).wait_send()
        for p in streams:
            for t in range(1, layers):
                pl.when(t > me_l)(lambda: acc_copy(p, t).start())

    out_ref[...] = jnp.transpose(att[...])

    for copy, cond in pending:
        if cond is None:
            copy.wait_send()
        else:
            pl.when(cond)(copy.wait_send)

    @pl.when(has_next)
    def _():
        for p in streams:
            for t in range(1, layers):
                @pl.when(t > me_l)
                def _():
                    acc_copy(p, t).wait_send()


def store(x_ref, f_ref, out_ref, feat_ref, sems):
    copies = [
        pltpu.make_async_copy(x_ref, out_ref, sems.at[0]),
        pltpu.make_async_copy(f_ref, feat_ref, sems.at[1]),
    ]
    for copy in copies:
        copy.start()
    for copy in copies:
        copy.wait()


def local(
    residual_in, attn_scale, mlp_scale, patterns, lengths, value_proj, out_proj, enc_weight, enc_bias,
    dec_weight, errors, clamp_mode, clamp_index, clamp_values, active_blocks,
):
    layers = lax.axis_size("layer")
    feat_n = lax.axis_size("feat")
    prompts, seq = patterns.shape[2], patterns.shape[3]
    head_dim, per_group = out_proj.shape[2], out_proj.shape[3]
    kv = value_proj.shape[3]
    rows, _, width = residual_in.shape
    block = enc_bias.shape[1]
    entries = clamp_values.shape[0]
    groups = lax.axis_size("groups")
    shares = groups if width % (16 * groups) == 0 else 1
    sizes = (layers, feat_n, seq, prompts, head_dim, per_group, kv, width, block, rows, entries, shares)
    x_in = residual_in[:, 0, :].T
    err_in = errors[0, :, 0, :].T
    pat_in = patterns[0]
    wv_in = value_proj[0, 0]
    wo_in = jnp.transpose(out_proj[0, :, :, :, 0, :], (0, 2, 3, 1))
    we_in = enc_weight[0, 0]
    wd_in = jnp.transpose(dec_weight[0, :, :, 0, :], (0, 2, 1))
    smem = pltpu.SMEM
    vmem = pl.BlockSpec(memory_space=pltpu.VMEM)
    hbm = pl.BlockSpec(memory_space=pl.ANY)
    small = (lengths, clamp_values, active_blocks, attn_scale, mlp_scale, enc_bias, clamp_mode, clamp_index)
    big = (x_in, err_in, pat_in, wv_in, wo_in, we_in, wd_in)
    half = seq // 2
    kv_heads = out_proj.shape[1]
    dma = pltpu.SemaphoreType.DMA
    out_t, out_f = pl.pallas_call(
        functools.partial(kernel, sizes),
        out_shape=(pltpu.VMEM((width, rows), F32), pltpu.VMEM((rows, block), BF16)),
        in_specs=[hbm] * 15,
        out_specs=(vmem, vmem),
        scratch_shapes=[(smem if i < 3 else pltpu.VMEM)(a.shape, a.dtype) for i, a in enumerate(small)]
        + [pltpu.VMEM(a.shape, a.dtype) for a in big]
        + [
            pltpu.VMEM((prompts, seq, width), F32),
            pltpu.VMEM((prompts, feat_n, seq, width), BF16),
            pltpu.VMEM((prompts, seq, width), BF16),
            pltpu.VMEM((rows, width), BF16),
            pltpu.VMEM((kv_heads, prompts, per_group * seq, seq), BF16),
            pltpu.VMEM((prompts, seq, kv), F32),
            pltpu.VMEM((prompts, seq, kv), F32),
            pltpu.VMEM((prompts, feat_n, seq, kv), BF16),
            pltpu.VMEM((prompts, 2, half, block), F32),
            pltpu.VMEM((prompts, 2 * feat_n, half, block), BF16),
            pltpu.VMEM((prompts, 2 * feat_n, half, block), BF16),
            pltpu.VMEM((prompts, 2 * feat_n, half, block), BF16),
            pltpu.VMEM((prompts, layers, seq, width), F32),
            pltpu.VMEM((prompts, layers, seq, width), F32),
            pltpu.VMEM((rows, width), F32),
            pltpu.VMEM((rows, width), F32),
        ]
        + [pltpu.VMEM((feat_n, width, block), BF16)] * 3
        + [
            dma((4,)), pltpu.SemaphoreType.REGULAR((2,)), dma((1,)), dma((prompts,)), dma((prompts, 2)), dma((prompts, feat_n)), dma((prompts,)),
            dma((prompts, feat_n)), dma((prompts, feat_n, 2)), dma((prompts,)), dma((prompts,)), dma((prompts, layers - 1)),
            dma((3, feat_n)), dma((shares, feat_n)),
        ],
        compiler_params=pltpu.CompilerParams(collective_id=0, has_side_effects=True),
    )(*small, *big)
    out_t, out_f = (pltpu.with_memory_space_constraint(a, pltpu.VMEM) for a in (out_t, out_f))
    out_t, out_f = pl.pallas_call(
        store,
        out_shape=(
            jax.ShapeDtypeStruct((width, rows), F32),
            jax.ShapeDtypeStruct((rows, block), BF16),
        ),
        in_specs=[vmem, vmem],
        out_specs=(hbm, hbm),
        scratch_shapes=[dma((2,))],
    )(out_t, out_f)
    return out_t.T[None, :, None, :], out_f[None]


def solution(mesh):
    return jax.shard_map(
        local,
        mesh=mesh,
        in_specs=(
            P("groups", "tok", "feat"),
            P("layer", "groups"),
            P("layer", "groups"),
            P("layer", None, "groups", None, None),
            P("groups"),
            P("layer", "tok", None, "feat"),
            P("layer", None, None, None, "tok", "feat"),
            P("layer", "tok", None, "feat"),
            P("layer", "feat"),
            P("layer", None, None, "tok", "feat"),
            P("layer", "groups", "tok", "feat"),
            P("layer", "feat"),
            P("layer", "feat"),
            P(),
            P("layer", "feat"),
        ),
        out_specs=(P("layer", "groups", "tok", "feat"), P("layer", "groups", "feat")),
        check_vma=False,
    )
```
